256 devices in a mesh: col: 32 (over x, z_hi, core), row: 8 (over y, z_lo).
Axes of the slice: x: 4, y: 4, z: 8 (z_hi: 4, z_lo: 2; z = z_hi * 2 + z_lo), core: 2. Of those that a mesh axis runs over, the one named last changes fastest.
Arguments:
- weight: bfloat16 [8192, 53248], P('row', 'col'), may hold values from -6 to 6
- factor: float32 [1664, 53248], P('row', 'col'), may hold values from -1 to 2, as said below
- keep_mask: int32 [64, 13], P('row'), may hold values 0 or 1
Outputs:
- pruned: bfloat16 [8192, 53248], P('row', 'col')
The draws below stay inside these ranges and needn't reach their ends.
Inputs may be any that keep to these rules, and one draw needn't show every extreme that they name: factor[i, k] = 0 for k < i; the diagonal entries factor[i, i] lie in [0.5, 2].
All inputs are finite; a program needn't handle non-finite values. No bound on the sum of `keep_mask` on one device may be relied on, other than what follows from the above.
Results may differ from the reference program's by a relative error of at most 0.0035.
Values may be sent and summed in bfloat16 or wider, within the bound.
No kernel may reach another device: no remote copies, remote signals or barrier semaphores. Data moves between devices by JAX's collectives and lax.ppermute only.
A program may use at most 192 MiB of HBM per device.

```python
import math
import jax
import jax.numpy as jnp
from jax import lax

ROWS = 8192
COLS = 53248
BLK = 128
PCOLS = 1664


def draw_factor(key, part):
    key_noise, key_pivot = jax.random.split(jax.random.fold_in(key, 7), 2)
    noise_draw = jnp.clip(jax.random.normal(key_noise, (PCOLS, COLS), jnp.float32), -6.0, 6.0)
    off_values = 0.4 * noise_draw / math.sqrt(PCOLS)
    pivot_values = jnp.exp(jax.random.uniform(key_pivot, (PCOLS, 1), jnp.float32, math.log(0.5), math.log(2.0)))
    row_ids = jnp.arange(PCOLS, dtype=jnp.int32)[:, None]
    col_ids = jnp.arange(COLS, dtype=jnp.int32)[None, :]
    factor_out = jnp.where(col_ids > row_ids, off_values, jnp.where(col_ids == row_ids, pivot_values, 0.0))
    return factor_out.astype(jnp.float32)


def set_ends(values, rng, smallest, largest):
    longest = values.shape.index(max(values.shape))
    spots = []
    for shift in (0, 1):
        where = [jax.random.randint(jax.random.fold_in(rng, axis), (), 0, length) for axis, length in enumerate(values.shape)]
        where[longest] = (where[longest] + shift) % values.shape[longest]
        spots.append(tuple(where))
    return values.at[spots[0]].set(smallest).at[spots[1]].set(largest)


def shard_levels(key, dims, cuts, least, top_value):
    def one(axis_at, blocks):
        draws = jax.random.uniform(jax.random.fold_in(jax.random.fold_in(key, 6), axis_at), (blocks,), jnp.float32, least / len(cuts), top_value / len(cuts))
        return jnp.repeat(jnp.exp(draws), dims[axis_at] // blocks).reshape((-1,) + (1,) * (len(dims) - axis_at - 1))

    loudness = one(*cuts[0])
    for cut in cuts[1:]:
        loudness = loudness * one(*cut)
    return loudness


def centred(key, shape, width, reach, pieces=(), held_as=jnp.bfloat16):
    array = width * jax.random.normal(key, shape, jnp.float32)
    if pieces:
        array = array * shard_levels(key, shape, pieces, -0.22, 0.18)
    return jnp.clip(array, -reach, reach).astype(held_as)


def setup_inputs(seed: int = 0) -> dict:
    arg_keys = jax.random.split(jax.random.key(seed), 4)
    return {
        "weight": centred(arg_keys[0], (ROWS, COLS), 1.0, 6.0, ((0, 8), (1, 32))),
        "factor": draw_factor(jax.random.fold_in(arg_keys[3], 71), 0),
        "keep_mask": set_ends((jax.random.randint(arg_keys[2], (ROWS // BLK, PCOLS // BLK), 0, 2) < 1).astype(jnp.int32), jax.random.fold_in(arg_keys[2], 1), 0, 1),
    }


def prune_block(block_weight, block_keep, block_factor):
    block_width = block_weight.shape[1]
    positions = jnp.arange(block_width, dtype=jnp.int32)

    def advance(column_at, carried):
        current, errors = carried
        column_at = jnp.asarray(column_at).astype(jnp.int32)
        column = lax.dynamic_slice_in_dim(current, column_at, 1, 1)
        keep_col = lax.dynamic_slice_in_dim(block_keep, column_at, 1, 1)
        factor_row = lax.dynamic_slice_in_dim(block_factor, column_at, 1, 0)
        pivot_value = jnp.sum(jnp.where(positions == column_at, factor_row[0], jnp.float32(0.0)))
        error_col = column * (1.0 - keep_col) / pivot_value
        later_mask = (positions > column_at)[None, :]
        current = current - jnp.where(later_mask, error_col * factor_row, jnp.float32(0.0))
        errors = errors + jnp.where((positions == column_at)[None, :], error_col, jnp.float32(0.0))
        return current, errors

    current, errors = lax.fori_loop(0, block_width, advance, (block_weight, jnp.zeros_like(block_weight)))
    return current * block_keep, errors


def reference(weight, factor, keep_mask):
    panel_w = weight[:, :PCOLS].astype(jnp.float32)
    keep_full = jnp.repeat(jnp.repeat(keep_mask.astype(jnp.float32), BLK, axis=0), BLK, axis=1)
    diag_block = factor[:, :PCOLS]
    kept_parts = []
    error_parts = []
    for block_id in range(PCOLS // BLK):
        low_col = block_id * BLK
        high_col = low_col + BLK
        kept_part, error_part = prune_block(panel_w[:, low_col:high_col], keep_full[:, low_col:high_col], diag_block[low_col:high_col, low_col:high_col])
        kept_parts.append(kept_part)
        error_parts.append(error_part)
        update = jnp.dot(error_part, diag_block[low_col:high_col, high_col:], precision=lax.Precision.HIGHEST)
        panel_w = jnp.concatenate([panel_w[:, :high_col], panel_w[:, high_col:] - update], axis=1)
    kept = jnp.concatenate(kept_parts, axis=1).astype(jnp.bfloat16)
    errors = jnp.concatenate(error_parts, axis=1)
    errors_low = lax.optimization_barrier(errors.astype(jnp.bfloat16)).astype(jnp.float32)
    rest_blocks = COLS // PCOLS - 1
    rest_weight = weight[:, PCOLS:].reshape(ROWS, rest_blocks, PCOLS).transpose(1, 0, 2)
    rest_factor = factor[:, PCOLS:].reshape(PCOLS, rest_blocks, PCOLS).transpose(1, 0, 2)

    def compensate(pair):
        block_weight, block_factor = pair
        factor_low = lax.optimization_barrier(block_factor.astype(jnp.bfloat16)).astype(jnp.float32)
        product = jnp.dot(errors_low, factor_low, precision=lax.Precision.HIGHEST)
        return (block_weight.astype(jnp.float32) - product).astype(jnp.bfloat16)

    rest_out = lax.map(compensate, (rest_weight, rest_factor))
    rest_out = rest_out.transpose(1, 0, 2).reshape(ROWS, COLS - PCOLS)
    return jnp.concatenate([kept, rest_out], axis=1)
```

```python
import jax
import jax.numpy as jnp
from jax import lax
from jax.experimental import pallas as pl
from jax.experimental.pallas import tpu as pltpu
from jax.sharding import PartitionSpec as P

BLK = 128
PCOLS = 1664
LANE_ROWS = 208
STRIP = 384
NBLK = PCOLS // BLK
ROWS_DEV = 1024
BF = jnp.bfloat16
F32 = jnp.float32


def strip_start(lane):
    return min((lane * LANE_ROWS // BLK) * BLK, PCOLS - STRIP)


def split(a):
    high = a.astype(BF)
    return high, (a - high.astype(F32)).astype(BF)


def mm_split(a, b):
    a_high, a_low = split(a)
    b_high, b_low = split(b)
    right = jnp.concatenate([b_high, b_low], axis=1)
    left = jnp.concatenate([a_high, a_low], axis=1)
    both = jnp.dot(left, jnp.concatenate([right, right], axis=0), preferred_element_type=F32)
    return both[:, :BLK] + both[:, BLK:]


def block_parts(block):
    parts = []
    at = block * BLK
    while at < (block + 1) * BLK:
        owner = at // LANE_ROWS
        stop = min((block + 1) * BLK, (owner + 1) * LANE_ROWS)
        parts.append((at, stop, block * BLK - strip_start(owner)))
        at = stop
    return parts


def inverse_kernel(strips_ref, out_ref, blocks_ref):
    for block in range(NBLK):
        for at, stop, offset in block_parts(block):
            low = at - block * BLK
            blocks_ref[block, low : low + stop - at, :] = strips_ref[at:stop, offset : offset + BLK]
    row = lax.broadcasted_iota(jnp.int32, (BLK, BLK), 0)
    column = lax.broadcasted_iota(jnp.int32, (BLK, BLK), 1)
    eye = (row == column).astype(F32)

    def one(block, carry):
        full = blocks_ref[block]
        on_diag = jnp.where(row == column, full, 0.0)
        pivot_col = jnp.sum(on_diag, axis=1, keepdims=True)
        pivot_row = jnp.sum(on_diag, axis=0, keepdims=True)
        strict = jnp.where(column > row, full, 0.0) / pivot_col
        near = jnp.where((row // 8) == (column // 8), strict, 0.0)
        near2 = mm_split(near, near)
        near4 = mm_split(near2, near2)
        inverse = mm_split(eye - near, eye + near2)
        inverse = mm_split(inverse, eye + near4)
        width = 8
        while width < BLK:
            pair = 2 * width
            off = jnp.where(((row // pair) == (column // pair)) & ((row // width) != (column // width)), strict, 0.0)
            inverse = inverse - mm_split(inverse, mm_split(off, inverse))
            width = pair
        high, low = split(inverse / pivot_row)
        start = pl.multiple_of(block * BLK, BLK)
        out_ref[pl.ds(start, BLK), :] = jnp.concatenate([high, low], axis=1)
        return carry

    lax.fori_loop(0, NBLK, one, 0)


def block_inverses(strips):
    return pl.pallas_call(
        inverse_kernel,
        out_shape=jax.ShapeDtypeStruct((PCOLS, 2 * BLK), BF),
        scratch_shapes=[pltpu.VMEM((NBLK, BLK, BLK), F32)],
        name="block_inverses",
    )(strips)


def prune_kernel(keep_ref, order_ref, weight_ref, *rest):
    pieces = rest[:8]
    inverse_ref, errors_ref, kept_ref, factor_ref = rest[8:]
    for place in range(8):
        start = pl.multiple_of(order_ref[place] * LANE_ROWS, 16)
        factor_ref[pl.ds(start, LANE_ROWS), :] = pieces[place][...]
    for low in range(0, PCOLS, 2 * BLK):
        width = min(2 * BLK, PCOLS - low)
        current = weight_ref[:, low : low + width].astype(F32)
        if low:
            current = current - jnp.dot(
                errors_ref[:, :low], factor_ref[:low, low : low + width], preferred_element_type=F32
            )
        for half in range(width // BLK):
            at = low + half * BLK
            part = current[:, half * BLK : (half + 1) * BLK]
            if half:
                part = part - jnp.dot(
                    errors_ref[:, low : low + BLK],
                    factor_ref[low : low + BLK, at : at + BLK],
                    preferred_element_type=F32,
                )
            high, lowpart = split(part)
            right = inverse_ref[at : at + BLK, :]
            both = jnp.dot(
                jnp.concatenate([high, lowpart], axis=1),
                jnp.concatenate([right, right], axis=0),
                preferred_element_type=F32,
            )
            solved = (both[:, :BLK] + both[:, BLK:]).astype(BF)
            for group in range(ROWS_DEV // BLK):
                top = group * BLK
                keep = keep_ref[group, at // BLK] > 0
                errors_ref[top : top + BLK, at : at + BLK] = jnp.where(
                    keep, jnp.zeros((BLK, BLK), BF), solved[top : top + BLK]
                )
                kept_ref[top : top + BLK, at : at + BLK] = jnp.where(
                    keep, high[top : top + BLK], jnp.zeros((BLK, BLK), BF)
                )


def prune(keep_mask, order, weight, pieces, inverses):
    vmem = pl.BlockSpec(memory_space=pltpu.VMEM)
    smem = pl.BlockSpec(memory_space=pltpu.SMEM)
    shape = jax.ShapeDtypeStruct((ROWS_DEV, PCOLS), BF)
    return pl.pallas_call(
        prune_kernel,
        in_specs=[smem, smem, vmem] + [vmem] * 8 + [vmem],
        out_specs=(vmem, vmem),
        out_shape=(shape, shape),
        scratch_shapes=[pltpu.VMEM((PCOLS, PCOLS), BF)],
        name="prune",
    )(keep_mask, order, weight, *pieces, inverses)


def col_at(x, zh, core):
    return (x % 4) * 8 + (zh % 4) * 2 + core


def row_at(y, zl):
    return (y % 4) * 2 + zl


def per_device(weight, factor, keep_mask):
    section = lax.axis_index("col")
    lane = lax.axis_index("row")
    x_at = section // 8
    zh_at = (section // 2) % 4
    core_at = section % 2
    factor_low = factor.astype(BF)

    starts = jnp.array([strip_start(k) for k in range(8)], jnp.int32)
    strip = lax.dynamic_slice(factor, (0, starts[lane]), (LANE_ROWS, STRIP))
    strips = lax.all_gather(strip, "row", axis=0, tiled=True)
    inverses = block_inverses(strips)

    pieces = [factor_low]
    order = [lane]
    for dy in range(4):
        for flip in (0, 1):
            if dy == 0 and flip == 0:
                continue
            pairs = [(row_at(y, zl), row_at(y + dy, zl ^ flip)) for y in range(4) for zl in (0, 1)]
            pieces.append(lax.ppermute(factor_low, ("col", "row"), pairs))
            order.append(row_at(lane // 2 - dy + 4, (lane % 2) ^ flip))
    errors, kept = prune(keep_mask, jnp.stack(order).astype(jnp.int32), weight, pieces, inverses)

    factor_all = lax.all_gather(factor_low, "row", axis=0, tiled=True)

    quarter = ROWS_DEV // 4
    half = quarter // 2
    mine = errors[:quarter]
    got = None
    for k in (1, 3, 2):
        sent = lax.ppermute(errors[k * quarter : (k + 1) * quarter], "col", [(0, col_at(k, 0, 0))])
        got = sent if got is None else got + sent
    own = jnp.where(x_at == 0, mine, got)
    up = lax.ppermute(own, "col", [(col_at(x, 0, 0), col_at(x, 1, 0)) for x in range(4)])
    down = lax.ppermute(own, "col", [(col_at(x, 0, 0), col_at(x, 3, 0)) for x in range(4)])
    far_a = lax.ppermute(up[:half], "col", [(col_at(x, 1, 0), col_at(x, 2, 0)) for x in range(4)])
    far_b = lax.ppermute(down[half:], "col", [(col_at(x, 3, 0), col_at(x, 2, 0)) for x in range(4)])
    own = jnp.where(zh_at == 0, own, up + down + jnp.concatenate([far_a, far_b], axis=0))
    places = [(x, z) for x in range(4) for z in range(4)]
    right = [(col_at(x, z, 0), col_at(x + 1, z, 0)) for x, z in places]
    left = [(col_at(x, z, 0), col_at(x - 1, z, 0)) for x, z in places]
    before = lax.ppermute(own, "col", right)
    after = lax.ppermute(own, "col", left)
    across_a = lax.ppermute(before[:half], "col", right)
    across_b = lax.ppermute(after[half:], "col", left)
    across = jnp.concatenate([across_a, across_b], axis=0)
    share = [(col_at(x, z, 0), col_at(x, z, 1)) for x, z in places]
    arrived = jnp.zeros((ROWS_DEV, PCOLS), BF)
    for shift, piece in ((0, own), (3, before), (1, after), (2, across)):
        both = jnp.where(core_at == 0, piece, lax.ppermute(piece, "col", share))
        arrived = lax.dynamic_update_slice(arrived, both, (((x_at + shift) % 4) * quarter, 0))

    compensation = jnp.dot(arrived, factor_all, preferred_element_type=F32)
    trailing = (weight.astype(F32) - compensation).astype(BF)
    return jnp.where(section == 0, kept, trailing)


def solution(mesh):
    in_specs = (P("row", "col"), P("row", "col"), P("row", None))
    out_specs = P("row", "col")
    return jax.shard_map(
        per_device, mesh=mesh, in_specs=in_specs, out_specs=out_specs, check_vma=False
    )
```

```python
import jax
import jax.numpy as jnp
from jax import lax
from jax.experimental import pallas as pl
from jax.experimental.pallas import tpu as pltpu
from jax.sharding import PartitionSpec as P

BLK = 128
PCOLS = 1664
LANES = 8
LANE_ROWS = 208
STRIP_BLOCKS = 3
PAD = 256
NBLK = PCOLS // BLK
ROWS_DEV = 1024
QUARTER = 256
HALF = 128
BF = jnp.bfloat16
F32 = jnp.float32


def split(a):
    high = a.astype(BF)
    return high, (a - high.astype(F32)).astype(BF)


def mm_split(a, b):
    right = jnp.concatenate(split(b), axis=1)
    left = jnp.concatenate(split(a), axis=1)
    both = jnp.dot(left, jnp.concatenate([right, right], axis=0), preferred_element_type=F32)
    return both[:, :BLK] + both[:, BLK:]


def triangle_inverses(fulls):
    row = lax.broadcasted_iota(jnp.int32, (BLK, BLK), 0)
    column = lax.broadcasted_iota(jnp.int32, (BLK, BLK), 1)
    eye = (row == column).astype(F32)
    stricts, pivots = [], []
    for full in fulls:
        on_diag = jnp.where(row == column, full, 0.0)
        pivots.append(jnp.sum(on_diag, axis=0, keepdims=True))
        stricts.append(jnp.where(column > row, full, 0.0) / jnp.sum(on_diag, axis=1, keepdims=True))
    nears = [jnp.where((row // 8) == (column // 8), strict, 0.0) for strict in stricts]
    near2s = [mm_split(near, near) for near in nears]
    near4s = [mm_split(near2, near2) for near2 in near2s]
    inverses = [mm_split(eye - near, eye + near2) for near, near2 in zip(nears, near2s)]
    inverses = [mm_split(inverse, eye + near4) for inverse, near4 in zip(inverses, near4s)]
    width = 8
    while width < BLK:
        pair = 2 * width
        inside = ((row // pair) == (column // pair)) & ((row // width) != (column // width))
        offs = [jnp.where(inside, strict, 0.0) for strict in stricts]
        steps = [mm_split(off, inverse) for off, inverse in zip(offs, inverses)]
        inverses = [inverse - mm_split(inverse, step) for inverse, step in zip(inverses, steps)]
        width = pair
    return [inverse / pivot for inverse, pivot in zip(inverses, pivots)]


def local_kernel(lane_ref, factor_ref, payload_ref, low_ref, rows_ref, inverse_ref):
    lane = lane_ref[0]
    first = jnp.minimum(lane * LANE_ROWS // BLK, NBLK - STRIP_BLOCKS)
    low = factor_ref[...].astype(BF)
    payload_ref[:, :PCOLS] = low
    low_ref[...] = low
    start = pl.multiple_of(first * BLK, BLK)
    rows_ref[PAD : PAD + LANE_ROWS, :] = factor_ref[:, pl.ds(start, STRIP_BLOCKS * BLK)]
    row = lax.broadcasted_iota(jnp.int32, (BLK, BLK), 0)
    column = lax.broadcasted_iota(jnp.int32, (BLK, BLK), 1)
    eye = (row == column).astype(F32)
    fulls, places = [], []
    for place in range(STRIP_BLOCKS):
        shift = (first + place) * BLK - lane * LANE_ROWS
        at = pl.multiple_of(shift + PAD, 16)
        valid = (row + shift >= 0) & (row + shift < LANE_ROWS)
        block = rows_ref[pl.ds(at, BLK), place * BLK : (place + 1) * BLK]
        fulls.append(jnp.where(valid, block, eye))
        places.append((at, valid))
    for (at, valid), inverse in zip(places, triangle_inverses(fulls)):
        here = inverse_ref[pl.ds(at, BLK), :]
        inverse_ref[pl.ds(at, BLK), :] = jnp.where(valid, inverse, here)
    high, lowpart = split(inverse_ref[PAD : PAD + LANE_ROWS, :])
    payload_ref[:, PCOLS : PCOLS + BLK] = high
    payload_ref[:, PCOLS + BLK :] = lowpart


def local_part(lane, factor):
    vmem = pl.BlockSpec(memory_space=pltpu.VMEM)
    smem = pl.BlockSpec(memory_space=pltpu.SMEM)
    return pl.pallas_call(
        local_kernel,
        in_specs=[smem, vmem],
        out_specs=(vmem, vmem),
        out_shape=(
            jax.ShapeDtypeStruct((LANE_ROWS, PCOLS + 2 * BLK), BF),
            jax.ShapeDtypeStruct((LANE_ROWS, PCOLS), BF),
        ),
        scratch_shapes=[
            pltpu.VMEM((PAD + LANE_ROWS + PAD, STRIP_BLOCKS * BLK), F32),
            pltpu.VMEM((PAD + LANE_ROWS + PAD, BLK), F32),
        ],
        name="local_part",
    )(lane, factor)


def prune_kernel(keep_ref, order_ref, weight_ref, *rest):
    pieces = rest[:LANES]
    errors_ref, kept_ref, factor_ref = rest[LANES:]
    for place in range(LANES):
        start = pl.multiple_of(order_ref[place] * LANE_ROWS, 16)
        factor_ref[pl.ds(start, LANE_ROWS), :] = pieces[place][...]
    row = lax.broadcasted_iota(jnp.int32, (BLK, BLK), 0)
    column = lax.broadcasted_iota(jnp.int32, (BLK, BLK), 1)
    eye = (row == column).astype(F32)
    for block in range(NBLK):
        at = block * BLK
        edge = (at // LANE_ROWS + 1) * LANE_ROWS - at
        if edge < BLK:
            stored = factor_ref[at : at + BLK, PCOLS:]
            whole = stored[:, :BLK].astype(F32) + stored[:, BLK:].astype(F32)
            top = jnp.where(row < edge, whole, eye)
            bottom = jnp.where(row < edge, eye, whole)
            factor_ref[at : at + BLK, PCOLS:] = jnp.concatenate(split(mm_split(top, bottom)), axis=1)
    for low in range(0, PCOLS, 2 * BLK):
        width = min(2 * BLK, PCOLS - low)
        current = weight_ref[:, low : low + width].astype(F32)
        if low:
            current = current - jnp.dot(
                errors_ref[:, :low], factor_ref[:low, low : low + width], preferred_element_type=F32
            )
        for half in range(width // BLK):
            at = low + half * BLK
            part = current[:, half * BLK : (half + 1) * BLK]
            if half:
                part = part - jnp.dot(
                    errors_ref[:, low : low + BLK],
                    factor_ref[low : low + BLK, at : at + BLK],
                    preferred_element_type=F32,
                )
            high, lowpart = split(part)
            right = factor_ref[at : at + BLK, PCOLS:]
            both = jnp.dot(
                jnp.concatenate([high, lowpart], axis=1),
                jnp.concatenate([right, right], axis=0),
                preferred_element_type=F32,
            )
            solved = (both[:, :BLK] + both[:, BLK:]).astype(BF)
            for group in range(ROWS_DEV // BLK):
                top = group * BLK
                keep = keep_ref[group, at // BLK] > 0
                errors_ref[top : top + BLK, at : at + BLK] = jnp.where(
                    keep, jnp.zeros((BLK, BLK), BF), solved[top : top + BLK]
                )
                kept_ref[top : top + BLK, at : at + BLK] = jnp.where(
                    keep, high[top : top + BLK], jnp.zeros((BLK, BLK), BF)
                )


def prune(keep_mask, order, weight, pieces):
    vmem = pl.BlockSpec(memory_space=pltpu.VMEM)
    smem = pl.BlockSpec(memory_space=pltpu.SMEM)
    shape = jax.ShapeDtypeStruct((ROWS_DEV, PCOLS), BF)
    return pl.pallas_call(
        prune_kernel,
        in_specs=[smem, smem, vmem] + [vmem] * LANES,
        out_specs=(vmem, vmem),
        out_shape=(shape, shape),
        scratch_shapes=[pltpu.VMEM((PCOLS, PCOLS + 2 * BLK), BF)],
        name="prune",
    )(keep_mask, order, weight, *pieces)


def finish_kernel(at_ref, owner_ref, piece_ref, factor_ref, weight_ref, kept_ref, before_ref, out_ref):
    product = jnp.dot(piece_ref[...], factor_ref[...], preferred_element_type=F32)
    trailing = (weight_ref[...].astype(F32) - product).astype(BF)
    out_ref[...] = jnp.where(owner_ref[0] > 0, kept_ref[...], trailing)


def finish(out, at, owner, piece, factor_all, weight, kept):
    rows = piece.shape[0]
    block = pl.BlockSpec((rows, PCOLS), lambda i, at_ref, owner_ref: (at_ref[0], 0))
    vmem = pl.BlockSpec(memory_space=pltpu.VMEM)
    return pl.pallas_call(
        finish_kernel,
        grid_spec=pltpu.PrefetchScalarGridSpec(
            num_scalar_prefetch=2,
            grid=(1,),
            in_specs=[vmem, vmem, block, block, pl.BlockSpec(memory_space=pl.ANY)],
            out_specs=block,
        ),
        out_shape=jax.ShapeDtypeStruct((ROWS_DEV, PCOLS), BF),
        input_output_aliases={6: 0},
        name="finish",
    )(at, owner, piece, factor_all, weight, kept, out)


def col_at(x, zh, core):
    return (x % 4) * 8 + (zh % 4) * 2 + core


def row_at(y, zl):
    return (y % 4) * 2 + zl


def vector(value):
    return jnp.reshape(value, (1,)).astype(jnp.int32)


def per_device(weight, factor, keep_mask):
    section = lax.axis_index("col")
    lane = lax.axis_index("row")
    x_at = section // 8
    zh_at = (section // 2) % 4
    core_at = section % 2
    payload, factor_low = local_part(vector(lane), factor)

    pieces = [payload]
    order = [lane]
    for dy in range(4):
        for flip in (0, 1):
            if dy == 0 and flip == 0:
                continue
            pairs = [(row_at(y, zl), row_at(y + dy, zl ^ flip)) for y in range(4) for zl in (0, 1)]
            pieces.append(lax.ppermute(payload, ("col", "row"), pairs))
            order.append(row_at(lane // 2 - dy + 4, (lane % 2) ^ flip))
    errors, kept = prune(keep_mask, jnp.stack(order).astype(jnp.int32), weight, pieces)

    factor_all = lax.all_gather(factor_low, "row", axis=0, tiled=True)

    mine = errors[:QUARTER]
    got = None
    for k in (1, 3, 2):
        sent = lax.ppermute(errors[k * QUARTER : (k + 1) * QUARTER], "col", [(0, col_at(k, 0, 0))])
        got = sent if got is None else got + sent
    own = jnp.where(x_at == 0, mine, got)
    up = lax.ppermute(own, "col", [(col_at(x, 0, 0), col_at(x, 1, 0)) for x in range(4)])
    down = lax.ppermute(own, "col", [(col_at(x, 0, 0), col_at(x, 3, 0)) for x in range(4)])
    far_a = lax.ppermute(up[:HALF], "col", [(col_at(x, 1, 0), col_at(x, 2, 0)) for x in range(4)])
    far_b = lax.ppermute(down[HALF:], "col", [(col_at(x, 3, 0), col_at(x, 2, 0)) for x in range(4)])
    own = jnp.where(zh_at == 0, own, up + down + jnp.concatenate([far_a, far_b], axis=0))

    places = [(x, z) for x in range(4) for z in range(4)]
    share = [(col_at(x, z, 0), col_at(x, z, 1)) for x, z in places]
    swap = [(col_at(x, z, c), col_at(x, z, 1 - c)) for x, z in places for c in (0, 1)]
    ring = [(col_at(x, z, 0), col_at(x + 1, z, 0)) for x, z in places]
    ring += [(col_at(x, z, 1), col_at(x - 1, z, 1)) for x, z in places]
    shared = lax.ppermute(own, "col", share)
    own = jnp.where(core_at == 0, own, shared)
    near = lax.ppermute(own, "col", ring)
    far = lax.ppermute(lax.dynamic_slice(near, (core_at * HALF, 0), (HALF, PCOLS)), "col", ring)
    near_other = lax.ppermute(near, "col", swap)
    far_other = lax.ppermute(far, "col", swap)

    owner = vector(section == 0)
    across = ((x_at + 2) % 4) * 2
    out = errors
    for at, piece in (
        (x_at, own),
        ((x_at + 3 - 2 * core_at) % 4, near),
        ((x_at + 1 + 2 * core_at) % 4, near_other),
        (across + core_at, far),
        (across + 1 - core_at, far_other),
    ):
        out = finish(out, vector(at), owner, piece, factor_all, weight, kept)
    return out


def solution(mesh):
    in_specs = (P("row", "col"), P("row", "col"), P("row", None))
    out_specs = P("row", "col")
    return jax.shard_map(
        per_device, mesh=mesh, in_specs=in_specs, out_specs=out_specs, check_vma=False
    )
```

```python
import jax
import jax.numpy as jnp
from jax import lax
from jax.experimental import pallas as pl
from jax.experimental.pallas import tpu as pltpu
from jax.sharding import PartitionSpec as P


BLK = 128
PCOLS = 1664
LANES = 8
LANE_ROWS = 208
STRIP_BLOCKS = 3
PAD = 256
NBLK = PCOLS // BLK
ROWS_DEV = 1024
QUARTER = 256
HALF = 128
BF = jnp.bfloat16
F32 = jnp.float32


def split(a):
    high = a.astype(BF)
    return high, (a - high.astype(F32)).astype(BF)


def mm_split(a, b):
    right = jnp.concatenate(split(b), axis=1)
    left = jnp.concatenate(split(a), axis=1)
    both = jnp.dot(left, jnp.concatenate([right, right], axis=0), preferred_element_type=F32)
    return both[:, :BLK] + both[:, BLK:]


def triangle_inverses(fulls):
    row = lax.broadcasted_iota(jnp.int32, (BLK, BLK), 0)
    column = lax.broadcasted_iota(jnp.int32, (BLK, BLK), 1)
    eye = (row == column).astype(F32)
    stricts, pivots = [], []
    for full in fulls:
        on_diag = jnp.where(row == column, full, 0.0)
        pivots.append(jnp.sum(on_diag, axis=0, keepdims=True))
        stricts.append(jnp.where(column > row, full, 0.0) / jnp.sum(on_diag, axis=1, keepdims=True))
    nears = [jnp.where((row // 8) == (column // 8), strict, 0.0) for strict in stricts]
    near2s = [mm_split(near, near) for near in nears]
    near4s = [mm_split(near2, near2) for near2 in near2s]
    inverses = [mm_split(eye - near, eye + near2) for near, near2 in zip(nears, near2s)]
    inverses = [mm_split(inverse, eye + near4) for inverse, near4 in zip(inverses, near4s)]
    width = 8
    while width < BLK:
        pair = 2 * width
        inside = ((row // pair) == (column // pair)) & ((row // width) != (column // width))
        offs = [jnp.where(inside, strict, 0.0) for strict in stricts]
        steps = [mm_split(off, inverse) for off, inverse in zip(offs, inverses)]
        inverses = [inverse - mm_split(inverse, step) for inverse, step in zip(inverses, steps)]
        width = pair
    return [inverse / pivot for inverse, pivot in zip(inverses, pivots)]


def local_kernel(lane_ref, factor_ref, payload_ref, low_ref, rows_ref, inverse_ref):
    lane = lane_ref[0]
    first = jnp.minimum(lane * LANE_ROWS // BLK, NBLK - STRIP_BLOCKS)
    low = factor_ref[...].astype(BF)
    payload_ref[:, :PCOLS] = low
    low_ref[...] = low
    start = pl.multiple_of(first * BLK, BLK)
    rows_ref[PAD : PAD + LANE_ROWS, :] = factor_ref[:, pl.ds(start, STRIP_BLOCKS * BLK)]
    row = lax.broadcasted_iota(jnp.int32, (BLK, BLK), 0)
    column = lax.broadcasted_iota(jnp.int32, (BLK, BLK), 1)
    eye = (row == column).astype(F32)
    fulls, places = [], []
    for place in range(STRIP_BLOCKS):
        shift = (first + place) * BLK - lane * LANE_ROWS
        at = pl.multiple_of(shift + PAD, 16)
        valid = (row + shift >= 0) & (row + shift < LANE_ROWS)
        block = rows_ref[pl.ds(at, BLK), place * BLK : (place + 1) * BLK]
        fulls.append(jnp.where(valid, block, eye))
        places.append((at, valid))
    for (at, valid), inverse in zip(places, triangle_inverses(fulls)):
        here = inverse_ref[pl.ds(at, BLK), :]
        inverse_ref[pl.ds(at, BLK), :] = jnp.where(valid, inverse, here)
    high, lowpart = split(inverse_ref[PAD : PAD + LANE_ROWS, :])
    payload_ref[:, PCOLS : PCOLS + BLK] = high
    payload_ref[:, PCOLS + BLK :] = lowpart


def local_part(lane, factor):
    vmem = pl.BlockSpec(memory_space=pltpu.VMEM)
    smem = pl.BlockSpec(memory_space=pltpu.SMEM)
    return pl.pallas_call(
        local_kernel,
        in_specs=[smem, vmem],
        out_specs=(vmem, vmem),
        out_shape=(
            jax.ShapeDtypeStruct((LANE_ROWS, PCOLS + 2 * BLK), BF),
            jax.ShapeDtypeStruct((LANE_ROWS, PCOLS), BF),
        ),
        scratch_shapes=[
            pltpu.VMEM((PAD + LANE_ROWS + PAD, STRIP_BLOCKS * BLK), F32),
            pltpu.VMEM((PAD + LANE_ROWS + PAD, BLK), F32),
        ],
        name="local_part",
    )(lane, factor)


def prune_kernel(keep_ref, order_ref, weight_ref, *rest):
    pieces = rest[:LANES]
    errors_ref, kept_ref, factor_ref = rest[LANES:]
    for place in range(LANES):
        start = pl.multiple_of(order_ref[place] * LANE_ROWS, 16)
        factor_ref[pl.ds(start, LANE_ROWS), :] = pieces[place][...]
    row = lax.broadcasted_iota(jnp.int32, (BLK, BLK), 0)
    column = lax.broadcasted_iota(jnp.int32, (BLK, BLK), 1)
    eye = (row == column).astype(F32)
    for block in range(NBLK):
        at = block * BLK
        edge = (at // LANE_ROWS + 1) * LANE_ROWS - at
        if edge < BLK:
            stored = factor_ref[at : at + BLK, PCOLS:]
            whole = stored[:, :BLK].astype(F32) + stored[:, BLK:].astype(F32)
            top = jnp.where(row < edge, whole, eye)
            bottom = jnp.where(row < edge, eye, whole)
            factor_ref[at : at + BLK, PCOLS:] = jnp.concatenate(split(mm_split(top, bottom)), axis=1)
    for low in range(0, PCOLS, 2 * BLK):
        width = min(2 * BLK, PCOLS - low)
        current = weight_ref[:, low : low + width].astype(F32)
        if low:
            current = current - jnp.dot(
                errors_ref[:, :low], factor_ref[:low, low : low + width], preferred_element_type=F32
            )
        for half in range(width // BLK):
            at = low + half * BLK
            part = current[:, half * BLK : (half + 1) * BLK]
            if half:
                part = part - jnp.dot(
                    errors_ref[:, low : low + BLK],
                    factor_ref[low : low + BLK, at : at + BLK],
                    preferred_element_type=F32,
                )
            high, lowpart = split(part)
            right = factor_ref[at : at + BLK, PCOLS:]
            both = jnp.dot(
                jnp.concatenate([high, lowpart], axis=1),
                jnp.concatenate([right, right], axis=0),
                preferred_element_type=F32,
            )
            solved = (both[:, :BLK] + both[:, BLK:]).astype(BF)
            for group in range(ROWS_DEV // BLK):
                top = group * BLK
                keep = keep_ref[group, at // BLK] > 0
                errors_ref[top : top + BLK, at : at + BLK] = jnp.where(
                    keep, jnp.zeros((BLK, BLK), BF), solved[top : top + BLK]
                )
                kept_ref[top : top + BLK, at : at + BLK] = jnp.where(
                    keep, high[top : top + BLK], jnp.zeros((BLK, BLK), BF)
                )


def prune(keep_mask, order, weight, pieces):
    vmem = pl.BlockSpec(memory_space=pltpu.VMEM)
    smem = pl.BlockSpec(memory_space=pltpu.SMEM)
    shape = jax.ShapeDtypeStruct((ROWS_DEV, PCOLS), BF)
    return pl.pallas_call(
        prune_kernel,
        in_specs=[smem, smem, vmem] + [vmem] * LANES,
        out_specs=(vmem, vmem),
        out_shape=(shape, shape),
        scratch_shapes=[pltpu.VMEM((PCOLS, PCOLS + 2 * BLK), BF)],
        name="prune",
    )(keep_mask, order, weight, *pieces)


def finish_kernel(at_ref, *rest):
    pieces = rest[:5]
    factor_ref, weight_ref, kept_ref, out_ref, errors_ref = rest[5:]
    step = pl.program_id(0)

    @pl.when(step == 0)
    def _():
        for place, piece in enumerate(pieces):
            start = pl.multiple_of(at_ref[place], HALF)
            errors_ref[pl.ds(start, piece.shape[0]), :] = piece[...]

    start = pl.multiple_of(step * QUARTER, QUARTER)
    product = jnp.dot(errors_ref[pl.ds(start, QUARTER), :], factor_ref[...], preferred_element_type=F32)
    trailing = (weight_ref[...].astype(F32) - product).astype(BF)
    out_ref[...] = jnp.where(at_ref[5] > 0, kept_ref[...], trailing)


def finish(at, pieces, factor_all, weight, kept):
    block = pl.BlockSpec((QUARTER, PCOLS), lambda i, at_ref: (i, 0))
    vmem = pl.BlockSpec(memory_space=pltpu.VMEM)
    return pl.pallas_call(
        finish_kernel,
        grid_spec=pltpu.PrefetchScalarGridSpec(
            num_scalar_prefetch=1,
            grid=(ROWS_DEV // QUARTER,),
            in_specs=[vmem] * 5 + [vmem, block, block],
            out_specs=block,
            scratch_shapes=[pltpu.VMEM((ROWS_DEV, PCOLS), BF)],
        ),
        out_shape=jax.ShapeDtypeStruct((ROWS_DEV, PCOLS), BF),
        name="finish",
    )(at, *pieces, factor_all, weight, kept)


def col_at(x, zh, core):
    return (x % 4) * 8 + (zh % 4) * 2 + core


def row_at(y, zl):
    return (y % 4) * 2 + zl


def vector(value):
    return jnp.reshape(value, (1,)).astype(jnp.int32)


def per_device(weight, factor, keep_mask):
    section = lax.axis_index("col")
    lane = lax.axis_index("row")
    x_at = section // 8
    zh_at = (section // 2) % 4
    core_at = section % 2
    payload, factor_low = local_part(vector(lane), factor)

    pieces = [payload]
    order = [lane]
    for dy in range(4):
        for flip in (0, 1):
            if dy == 0 and flip == 0:
                continue
            pairs = [(row_at(y, zl), row_at(y + dy, zl ^ flip)) for y in range(4) for zl in (0, 1)]
            pieces.append(lax.ppermute(payload, ("col", "row"), pairs))
            order.append(row_at(lane // 2 - dy + 4, (lane % 2) ^ flip))
    errors, kept = prune(keep_mask, jnp.stack(order).astype(jnp.int32), weight, pieces)

    flipped = [(row_at(y, zl), row_at(y, 1 - zl)) for y in range(4) for zl in (0, 1)]
    partner = lax.ppermute(factor_low, "row", flipped)
    even = lane % 2 == 0
    pair = jnp.concatenate(
        [jnp.where(even, factor_low, partner), jnp.where(even, partner, factor_low)], axis=0
    )
    groups = [[row_at(y, zl) for y in range(4)] for zl in (0, 1)]
    factor_all = lax.all_gather(pair, "row", axis=0, tiled=True, axis_index_groups=groups)

    mine = errors[:QUARTER]
    got = None
    for k in (1, 3, 2):
        sent = lax.ppermute(errors[k * QUARTER : (k + 1) * QUARTER], "col", [(0, col_at(k, 0, 0))])
        got = sent if got is None else got + sent
    own = jnp.where(x_at == 0, mine, got)
    up = lax.ppermute(own, "col", [(col_at(x, 0, 0), col_at(x, 1, 0)) for x in range(4)])
    down = lax.ppermute(own, "col", [(col_at(x, 0, 0), col_at(x, 3, 0)) for x in range(4)])
    far_a = lax.ppermute(up[:HALF], "col", [(col_at(x, 1, 0), col_at(x, 2, 0)) for x in range(4)])
    far_b = lax.ppermute(down[HALF:], "col", [(col_at(x, 3, 0), col_at(x, 2, 0)) for x in range(4)])
    own = jnp.where(zh_at == 0, own, up + down + jnp.concatenate([far_a, far_b], axis=0))

    places = [(x, z) for x in range(4) for z in range(4)]
    share = [(col_at(x, z, 0), col_at(x, z, 1)) for x, z in places]
    swap = [(col_at(x, z, c), col_at(x, z, 1 - c)) for x, z in places for c in (0, 1)]
    ring = [(col_at(x, z, 0), col_at(x + 1, z, 0)) for x, z in places]
    ring += [(col_at(x, z, 1), col_at(x - 1, z, 1)) for x, z in places]
    shared = lax.ppermute(own, "col", share)
    own = jnp.where(core_at == 0, own, shared)
    near = lax.ppermute(own, "col", ring)
    far = lax.ppermute(lax.dynamic_slice(near, (core_at * HALF, 0), (HALF, PCOLS)), "col", ring)
    near_other = lax.ppermute(near, "col", swap)
    far_other = lax.ppermute(far, "col", swap)

    across = ((x_at + 2) % 4) * QUARTER
    at = jnp.stack(
        [
            x_at * QUARTER,
            ((x_at + 3 - 2 * core_at) % 4) * QUARTER,
            ((x_at + 1 + 2 * core_at) % 4) * QUARTER,
            across + core_at * HALF,
            across + (1 - core_at) * HALF,
            (section == 0).astype(jnp.int32),
        ]
    ).astype(jnp.int32)
    return finish(at, (own, near, near_other, far, far_other), factor_all, weight, kept)


def solution(mesh):
    in_specs = (P("row", "col"), P("row", "col"), P("row", None))
    out_specs = P("row", "col")
    return jax.shard_map(
        per_device, mesh=mesh, in_specs=in_specs, out_specs=out_specs, check_vma=False
    )
```

```python
import jax
import jax.numpy as jnp
from jax import lax
from jax.experimental import pallas as pl
from jax.experimental.pallas import tpu as pltpu
from jax.sharding import PartitionSpec as P


BLK = 128
PCOLS = 1664
LANES = 8
LANE_ROWS = 208
STRIP_BLOCKS = 3
PAD = 256
NBLK = PCOLS // BLK
ROWS_DEV = 1024
QUARTER = 256
HALF = 128
BF = jnp.bfloat16
F32 = jnp.float32


def split(a):
    high = a.astype(BF)
    return high, (a - high.astype(F32)).astype(BF)


def mm_split(a, b):
    right = jnp.concatenate(split(b), axis=1)
    left = jnp.concatenate(split(a), axis=1)
    both = jnp.dot(left, jnp.concatenate([right, right], axis=0), preferred_element_type=F32)
    return both[:, :BLK] + both[:, BLK:]


def triangle_inverses(fulls):
    row = lax.broadcasted_iota(jnp.int32, (BLK, BLK), 0)
    column = lax.broadcasted_iota(jnp.int32, (BLK, BLK), 1)
    eye = (row == column).astype(F32)
    stricts, pivots = [], []
    for full in fulls:
        on_diag = jnp.where(row == column, full, 0.0)
        pivots.append(jnp.sum(on_diag, axis=0, keepdims=True))
        stricts.append(jnp.where(column > row, full, 0.0) / jnp.sum(on_diag, axis=1, keepdims=True))
    nears = [jnp.where((row // 8) == (column // 8), strict, 0.0) for strict in stricts]
    near2s = [mm_split(near, near) for near in nears]
    near4s = [mm_split(near2, near2) for near2 in near2s]
    inverses = [mm_split(eye - near, eye + near2) for near, near2 in zip(nears, near2s)]
    inverses = [mm_split(inverse, eye + near4) for inverse, near4 in zip(inverses, near4s)]
    width = 8
    while width < BLK:
        pair = 2 * width
        inside = ((row // pair) == (column // pair)) & ((row // width) != (column // width))
        offs = [jnp.where(inside, strict, 0.0) for strict in stricts]
        steps = [mm_split(off, inverse) for off, inverse in zip(offs, inverses)]
        inverses = [inverse - mm_split(inverse, step) for inverse, step in zip(inverses, steps)]
        width = pair
    return [inverse / pivot for inverse, pivot in zip(inverses, pivots)]


def local_kernel(lane_ref, factor_ref, payload_ref, low_ref, rows_ref, inverse_ref):
    lane = lane_ref[0]
    first = jnp.minimum(lane * LANE_ROWS // BLK, NBLK - STRIP_BLOCKS)
    low = factor_ref[...].astype(BF)
    payload_ref[:, :PCOLS] = low
    low_ref[...] = low
    start = pl.multiple_of(first * BLK, BLK)
    rows_ref[PAD : PAD + LANE_ROWS, :] = factor_ref[:, pl.ds(start, STRIP_BLOCKS * BLK)]
    row = lax.broadcasted_iota(jnp.int32, (BLK, BLK), 0)
    column = lax.broadcasted_iota(jnp.int32, (BLK, BLK), 1)
    eye = (row == column).astype(F32)
    fulls, places = [], []
    for place in range(STRIP_BLOCKS):
        shift = (first + place) * BLK - lane * LANE_ROWS
        at = pl.multiple_of(shift + PAD, 16)
        valid = (row + shift >= 0) & (row + shift < LANE_ROWS)
        block = rows_ref[pl.ds(at, BLK), place * BLK : (place + 1) * BLK]
        fulls.append(jnp.where(valid, block, eye))
        places.append((at, valid))
    for (at, valid), inverse in zip(places, triangle_inverses(fulls)):
        here = inverse_ref[pl.ds(at, BLK), :]
        inverse_ref[pl.ds(at, BLK), :] = jnp.where(valid, inverse, here)
    high, lowpart = split(inverse_ref[PAD : PAD + LANE_ROWS, :])
    payload_ref[:, PCOLS : PCOLS + BLK] = high
    payload_ref[:, PCOLS + BLK :] = lowpart


def local_part(lane, factor):
    vmem = pl.BlockSpec(memory_space=pltpu.VMEM)
    smem = pl.BlockSpec(memory_space=pltpu.SMEM)
    return pl.pallas_call(
        local_kernel,
        in_specs=[smem, vmem],
        out_specs=(vmem, vmem),
        out_shape=(
            jax.ShapeDtypeStruct((LANE_ROWS, PCOLS + 2 * BLK), BF),
            jax.ShapeDtypeStruct((LANE_ROWS, PCOLS), BF),
        ),
        scratch_shapes=[
            pltpu.VMEM((PAD + LANE_ROWS + PAD, STRIP_BLOCKS * BLK), F32),
            pltpu.VMEM((PAD + LANE_ROWS + PAD, BLK), F32),
        ],
        name="local_part",
    )(lane, factor)


def prune_kernel(keep_ref, order_ref, weight_ref, *rest):
    pieces = rest[:LANES]
    quarter_refs = rest[LANES : LANES + 4]
    kept_ref, factor_ref, errors_ref = rest[LANES + 4 :]
    for place in range(LANES):
        start = pl.multiple_of(order_ref[place] * LANE_ROWS, 16)
        factor_ref[pl.ds(start, LANE_ROWS), :] = pieces[place][...]
    row = lax.broadcasted_iota(jnp.int32, (BLK, BLK), 0)
    column = lax.broadcasted_iota(jnp.int32, (BLK, BLK), 1)
    eye = (row == column).astype(F32)
    for block in range(NBLK):
        at = block * BLK
        edge = (at // LANE_ROWS + 1) * LANE_ROWS - at
        if edge < BLK:
            stored = factor_ref[at : at + BLK, PCOLS:]
            whole = stored[:, :BLK].astype(F32) + stored[:, BLK:].astype(F32)
            top = jnp.where(row < edge, whole, eye)
            bottom = jnp.where(row < edge, eye, whole)
            factor_ref[at : at + BLK, PCOLS:] = jnp.concatenate(split(mm_split(top, bottom)), axis=1)
    for low in range(0, PCOLS, 2 * BLK):
        width = min(2 * BLK, PCOLS - low)
        current = weight_ref[:, low : low + width].astype(F32)
        if low:
            current = current - jnp.dot(
                errors_ref[:, :low], factor_ref[:low, low : low + width], preferred_element_type=F32
            )
        for half in range(width // BLK):
            at = low + half * BLK
            part = current[:, half * BLK : (half + 1) * BLK]
            if half:
                part = part - jnp.dot(
                    errors_ref[:, low : low + BLK],
                    factor_ref[low : low + BLK, at : at + BLK],
                    preferred_element_type=F32,
                )
            high, lowpart = split(part)
            right = factor_ref[at : at + BLK, PCOLS:]
            both = jnp.dot(
                jnp.concatenate([high, lowpart], axis=1),
                jnp.concatenate([right, right], axis=0),
                preferred_element_type=F32,
            )
            solved = (both[:, :BLK] + both[:, BLK:]).astype(BF)
            for group in range(ROWS_DEV // BLK):
                top = group * BLK
                keep = keep_ref[group, at // BLK] > 0
                error = jnp.where(keep, jnp.zeros((BLK, BLK), BF), solved[top : top + BLK])
                errors_ref[top : top + BLK, at : at + BLK] = error
                inner = top % QUARTER
                quarter_refs[top // QUARTER][inner : inner + BLK, at : at + BLK] = error
                kept_ref[top : top + BLK, at : at + BLK] = jnp.where(
                    keep, high[top : top + BLK], jnp.zeros((BLK, BLK), BF)
                )


def prune(keep_mask, order, weight, pieces):
    vmem = pl.BlockSpec(memory_space=pltpu.VMEM)
    smem = pl.BlockSpec(memory_space=pltpu.SMEM)
    quarter = jax.ShapeDtypeStruct((QUARTER, PCOLS), BF)
    return pl.pallas_call(
        prune_kernel,
        in_specs=[smem, smem, vmem] + [vmem] * LANES,
        out_specs=(vmem,) * 5,
        out_shape=(quarter,) * 4 + (jax.ShapeDtypeStruct((ROWS_DEV, PCOLS), BF),),
        scratch_shapes=[
            pltpu.VMEM((PCOLS, PCOLS + 2 * BLK), BF),
            pltpu.VMEM((ROWS_DEV, PCOLS), BF),
        ],
        name="prune",
    )(keep_mask, order, weight, *pieces)


def subtract(piece, factor, weight_ref, kept_ref, owner):
    product = jnp.dot(piece, factor, preferred_element_type=F32)
    trailing = (weight_ref[...].astype(F32) - product).astype(BF)
    return jnp.where(owner > 0, kept_ref[...], trailing)


def own_kernel(at_ref, piece_ref, *rest):
    parts = rest[:5]
    weight_ref, kept_ref, out_ref, factor_ref = rest[5:]
    for place, part in enumerate(parts):
        start = pl.multiple_of(at_ref[2 + place] * LANE_ROWS, 16)
        factor_ref[pl.ds(start, part.shape[0]), :] = part[...]
    out_ref[...] = subtract(piece_ref[...], factor_ref[...], weight_ref, kept_ref, at_ref[1])


def near_kernel(at_ref, first_ref, second_ref, factor_ref, weight_ref, kept_ref, out_ref):
    for step, piece_ref in enumerate((first_ref, second_ref)):

        @pl.when(pl.program_id(0) == step)
        def _():
            out_ref[...] = subtract(piece_ref[...], factor_ref[...], weight_ref, kept_ref, at_ref[2])


def far_kernel(at_ref, first_ref, second_ref, factor_ref, weight_ref, kept_ref, out_ref, piece_ref):
    for place, half_ref in enumerate((first_ref, second_ref)):
        start = pl.multiple_of(at_ref[2 + place] * HALF, HALF)
        piece_ref[pl.ds(start, HALF), :] = half_ref[...]
    out_ref[...] = subtract(piece_ref[...], factor_ref[...], weight_ref, kept_ref, at_ref[1])


def finish(kernel, steps, at, inputs, weight, kept, extra=None, scratch=()):
    block = pl.BlockSpec((QUARTER, PCOLS), lambda i, at_ref: (at_ref[i], 0))
    vmem = pl.BlockSpec(memory_space=pltpu.VMEM)
    out_shape = [jax.ShapeDtypeStruct((ROWS_DEV, PCOLS), BF)]
    if extra is not None:
        out_shape.append(extra)
    return pl.pallas_call(
        kernel,
        grid_spec=pltpu.PrefetchScalarGridSpec(
            num_scalar_prefetch=1,
            grid=(steps,),
            in_specs=[vmem] * len(inputs) + [block, block],
            out_specs=[block] + [vmem] * (len(out_shape) - 1),
            scratch_shapes=list(scratch),
        ),
        out_shape=out_shape,
        input_output_aliases={len(inputs) + 2: 0},
    )(at, *inputs, weight, kept)


def col_at(x, zh, core):
    return (x % 4) * 8 + (zh % 4) * 2 + core


def row_at(y, zl):
    return (y % 4) * 2 + zl


def vector(value):
    return jnp.reshape(value, (1,)).astype(jnp.int32)


def per_device(weight, factor, keep_mask):
    section = lax.axis_index("col")
    lane = lax.axis_index("row")
    x_at = section // 8
    zh_at = (section // 2) % 4
    core_at = section % 2
    payload, factor_low = local_part(vector(lane), factor)

    def hop(array, dy, flip):
        pairs = [(row_at(y, zl), row_at(y + dy, zl ^ flip)) for y in range(4) for zl in (0, 1)]
        return lax.ppermute(array, ("col", "row"), pairs)

    y_at, zl_at = lane // 2, lane % 2
    up_same = hop(payload, 1, 0)
    down_other = hop(payload, 3, 1)
    up_other = hop(payload, 1, 1)
    down_same = hop(payload, 3, 0)
    other = hop(payload, 0, 1)
    far_same = hop(up_same, 1, 0)
    far_other = hop(down_other, 3, 0)
    pieces = [payload, up_same, down_other, up_other, down_same, other, far_same, far_other]
    order = [
        lane,
        row_at(y_at + 3, zl_at),
        row_at(y_at + 1, 1 - zl_at),
        row_at(y_at + 3, 1 - zl_at),
        row_at(y_at + 1, zl_at),
        row_at(y_at, 1 - zl_at),
        row_at(y_at + 2, zl_at),
        row_at(y_at + 2, 1 - zl_at),
    ]
    *quarters, kept = prune(keep_mask, jnp.stack(order).astype(jnp.int32), weight, pieces)

    def along(array, dy):
        return lax.ppermute(array, "row", [(row_at(y, zl), row_at(y + dy, zl)) for y in range(4) for zl in (0, 1)])

    partner = lax.ppermute(factor_low, "row", [(k, k ^ 1) for k in range(LANES)])
    even = zl_at == 0
    pair = jnp.concatenate(
        [jnp.where(even, factor_low, partner), jnp.where(even, partner, factor_low)], axis=0
    )
    pair_up = along(pair, 1)
    pair_down = along(pair, 3)
    far_even = along(pair_up[:LANE_ROWS], 1)
    far_odd = along(pair_down[LANE_ROWS:], 3)
    parts = (pair, pair_up, pair_down, far_even, far_odd)
    part_rows = [
        row_at(y_at, 0), row_at(y_at + 3, 0), row_at(y_at + 1, 0), row_at(y_at + 2, 0), row_at(y_at + 2, 1)
    ]

    got = None
    for k in (2, 1, 3):
        sent = lax.ppermute(quarters[k], "col", [(0, col_at(k, 0, 0))])
        got = sent if got is None else got + sent
    own = jnp.where(x_at == 0, quarters[0], got)
    up = lax.ppermute(own, "col", [(col_at(x, 0, 0), col_at(x, 1, 0)) for x in range(4)])
    down = lax.ppermute(own, "col", [(col_at(x, 0, 0), col_at(x, 3, 0)) for x in range(4)])
    far_a = lax.ppermute(up[:HALF], "col", [(col_at(x, 1, 0), col_at(x, 2, 0)) for x in range(4)])
    far_b = lax.ppermute(down[HALF:], "col", [(col_at(x, 3, 0), col_at(x, 2, 0)) for x in range(4)])
    own = jnp.where(zh_at == 0, own, up + down + jnp.concatenate([far_a, far_b], axis=0))

    places = [(x, z) for x in range(4) for z in range(4)]
    share = [(col_at(x, z, 0), col_at(x, z, 1)) for x, z in places]
    swap = [(col_at(x, z, c), col_at(x, z, 1 - c)) for x, z in places for c in (0, 1)]
    ring = [(col_at(x, z, 0), col_at(x + 1, z, 0)) for x, z in places]
    ring += [(col_at(x, z, 1), col_at(x - 1, z, 1)) for x, z in places]
    shared = lax.ppermute(own, "col", share)
    own = jnp.where(core_at == 0, own, shared)
    near = lax.ppermute(own, "col", ring)
    far = lax.ppermute(lax.dynamic_slice(near, (core_at * HALF, 0), (HALF, PCOLS)), "col", ring)
    near_other = lax.ppermute(near, "col", swap)
    far_other = lax.ppermute(far, "col", swap)

    def ints(*values):
        return jnp.stack(values).astype(jnp.int32)

    owner = section == 0
    factor_shape = jax.ShapeDtypeStruct((PCOLS, PCOLS), BF)
    out, factor_all = finish(own_kernel, 1, ints(x_at, owner, *part_rows), (own, *parts), weight, kept, factor_shape)
    ways = ints((x_at + 3 - 2 * core_at) % 4, (x_at + 1 + 2 * core_at) % 4, owner)
    (out,) = finish(near_kernel, 2, ways, (near, near_other, factor_all), weight, out)
    (out,) = finish(
        far_kernel,
        1,
        ints((x_at + 2) % 4, owner, core_at, 1 - core_at),
        (far, far_other, factor_all),
        weight,
        out,
        scratch=[pltpu.VMEM((QUARTER, PCOLS), BF)],
    )
    return out


def solution(mesh):
    in_specs = (P("row", "col"), P("row", "col"), P("row", None))
    out_specs = P("row", "col")
    return jax.shard_map(per_device, mesh=mesh, in_specs=in_specs, out_specs=out_specs, check_vma=False)
```

```python
import jax
import jax.numpy as jnp
from jax import lax
from jax.experimental import pallas as pl
from jax.experimental.pallas import tpu as pltpu
from jax.sharding import PartitionSpec as P


BLK = 128
PCOLS = 1664
LANES = 8
LANE_ROWS = 208
STRIP_BLOCKS = 3
PAD = 256
NBLK = PCOLS // BLK
ROWS_DEV = 1024
QUARTER = 256
HALF = 128
BF = jnp.bfloat16
F32 = jnp.float32


def split(a):
    high = a.astype(BF)
    return high, (a - high.astype(F32)).astype(BF)


def mm_split(a, b):
    right = jnp.concatenate(split(b), axis=1)
    left = jnp.concatenate(split(a), axis=1)
    both = jnp.dot(left, jnp.concatenate([right, right], axis=0), preferred_element_type=F32)
    return both[:, :BLK] + both[:, BLK:]


def triangle_inverses(fulls):
    row = lax.broadcasted_iota(jnp.int32, (BLK, BLK), 0)
    column = lax.broadcasted_iota(jnp.int32, (BLK, BLK), 1)
    eye = (row == column).astype(F32)
    stricts, pivots = [], []
    for full in fulls:
        on_diag = jnp.where(row == column, full, 0.0)
        pivots.append(jnp.sum(on_diag, axis=0, keepdims=True))
        stricts.append(jnp.where(column > row, full, 0.0) / jnp.sum(on_diag, axis=1, keepdims=True))
    nears = [jnp.where((row // 8) == (column // 8), strict, 0.0) for strict in stricts]
    near2s = [mm_split(near, near) for near in nears]
    near4s = [mm_split(near2, near2) for near2 in near2s]
    inverses = [mm_split(eye - near, eye + near2) for near, near2 in zip(nears, near2s)]
    inverses = [mm_split(inverse, eye + near4) for inverse, near4 in zip(inverses, near4s)]
    width = 8
    while width < BLK:
        pair = 2 * width
        inside = ((row // pair) == (column // pair)) & ((row // width) != (column // width))
        offs = [jnp.where(inside, strict, 0.0) for strict in stricts]
        steps = [mm_split(off, inverse) for off, inverse in zip(offs, inverses)]
        inverses = [inverse - mm_split(inverse, step) for inverse, step in zip(inverses, steps)]
        width = pair
    return [inverse / pivot for inverse, pivot in zip(inverses, pivots)]


def local_kernel(lane_ref, factor_ref, payload_ref, low_ref, rows_ref, inverse_ref):
    lane = lane_ref[0]
    first = jnp.minimum(lane * LANE_ROWS // BLK, NBLK - STRIP_BLOCKS)
    low = factor_ref[...].astype(BF)
    payload_ref[:, :PCOLS] = low
    low_ref[...] = low
    start = pl.multiple_of(first * BLK, BLK)
    rows_ref[PAD : PAD + LANE_ROWS, :] = factor_ref[:, pl.ds(start, STRIP_BLOCKS * BLK)]
    row = lax.broadcasted_iota(jnp.int32, (BLK, BLK), 0)
    column = lax.broadcasted_iota(jnp.int32, (BLK, BLK), 1)
    eye = (row == column).astype(F32)
    fulls, places = [], []
    for place in range(STRIP_BLOCKS):
        shift = (first + place) * BLK - lane * LANE_ROWS
        at = pl.multiple_of(shift + PAD, 16)
        valid = (row + shift >= 0) & (row + shift < LANE_ROWS)
        block = rows_ref[pl.ds(at, BLK), place * BLK : (place + 1) * BLK]
        fulls.append(jnp.where(valid, block, eye))
        places.append((at, valid))
    for (at, valid), inverse in zip(places, triangle_inverses(fulls)):
        here = inverse_ref[pl.ds(at, BLK), :]
        inverse_ref[pl.ds(at, BLK), :] = jnp.where(valid, inverse, here)
    high, lowpart = split(inverse_ref[PAD : PAD + LANE_ROWS, :])
    payload_ref[:, PCOLS : PCOLS + BLK] = high
    payload_ref[:, PCOLS + BLK :] = lowpart


def local_part(lane, factor):
    vmem = pl.BlockSpec(memory_space=pltpu.VMEM)
    smem = pl.BlockSpec(memory_space=pltpu.SMEM)
    return pl.pallas_call(
        local_kernel,
        in_specs=[smem, vmem],
        out_specs=(vmem, vmem),
        out_shape=(
            jax.ShapeDtypeStruct((LANE_ROWS, PCOLS + 2 * BLK), BF),
            jax.ShapeDtypeStruct((LANE_ROWS, PCOLS), BF),
        ),
        scratch_shapes=[
            pltpu.VMEM((PAD + LANE_ROWS + PAD, STRIP_BLOCKS * BLK), F32),
            pltpu.VMEM((PAD + LANE_ROWS + PAD, BLK), F32),
        ],
        name="local_part",
    )(lane, factor)


def prune_kernel(keep_ref, order_ref, weight_ref, *rest):
    pieces = rest[:LANES]
    quarter_refs = rest[LANES : LANES + 4]
    kept_ref, factor_ref, errors_ref = rest[LANES + 4 :]
    for place in range(LANES):
        start = pl.multiple_of(order_ref[place] * LANE_ROWS, 16)
        factor_ref[pl.ds(start, LANE_ROWS), :] = pieces[place][...]
    row = lax.broadcasted_iota(jnp.int32, (BLK, BLK), 0)
    column = lax.broadcasted_iota(jnp.int32, (BLK, BLK), 1)
    eye = (row == column).astype(F32)
    for block in range(NBLK):
        at = block * BLK
        edge = (at // LANE_ROWS + 1) * LANE_ROWS - at
        if edge < BLK:
            stored = factor_ref[at : at + BLK, PCOLS:]
            whole = stored[:, :BLK].astype(F32) + stored[:, BLK:].astype(F32)
            top = jnp.where(row < edge, whole, eye)
            bottom = jnp.where(row < edge, eye, whole)
            factor_ref[at : at + BLK, PCOLS:] = jnp.concatenate(split(mm_split(top, bottom)), axis=1)
    for low in range(0, PCOLS, 2 * BLK):
        width = min(2 * BLK, PCOLS - low)
        current = weight_ref[:, low : low + width].astype(F32)
        if low:
            current = current - jnp.dot(
                errors_ref[:, :low], factor_ref[:low, low : low + width], preferred_element_type=F32
            )
        for half in range(width // BLK):
            at = low + half * BLK
            part = current[:, half * BLK : (half + 1) * BLK]
            if half:
                part = part - jnp.dot(
                    errors_ref[:, low : low + BLK],
                    factor_ref[low : low + BLK, at : at + BLK],
                    preferred_element_type=F32,
                )
            high, lowpart = split(part)
            right = factor_ref[at : at + BLK, PCOLS:]
            both = jnp.dot(
                jnp.concatenate([high, lowpart], axis=1),
                jnp.concatenate([right, right], axis=0),
                preferred_element_type=F32,
            )
            solved = (both[:, :BLK] + both[:, BLK:]).astype(BF)
            for group in range(ROWS_DEV // BLK):
                top = group * BLK
                keep = keep_ref[group, at // BLK] > 0
                error = jnp.where(keep, jnp.zeros((BLK, BLK), BF), solved[top : top + BLK])
                errors_ref[top : top + BLK, at : at + BLK] = error
                inner = top % QUARTER
                quarter_refs[top // QUARTER][inner : inner + BLK, at : at + BLK] = error
                kept_ref[top : top + BLK, at : at + BLK] = jnp.where(
                    keep, high[top : top + BLK], jnp.zeros((BLK, BLK), BF)
                )


def prune(keep_mask, order, weight, pieces):
    vmem = pl.BlockSpec(memory_space=pltpu.VMEM)
    smem = pl.BlockSpec(memory_space=pltpu.SMEM)
    quarter = pltpu.VMEM((QUARTER, PCOLS), BF)
    return pl.pallas_call(
        prune_kernel,
        in_specs=[smem, smem, vmem] + [vmem] * LANES,
        out_specs=(vmem,) * 5,
        out_shape=(quarter,) * 4 + (jax.ShapeDtypeStruct((ROWS_DEV, PCOLS), BF),),
        scratch_shapes=[
            pltpu.VMEM((PCOLS, PCOLS + 2 * BLK), BF),
            pltpu.VMEM((ROWS_DEV, PCOLS), BF),
        ],
        compiler_params=pltpu.CompilerParams(vmem_limit_bytes=36 * 2**20),
        name="prune",
    )(keep_mask, order, weight, *pieces)


def subtract(piece, factor, weight_ref, kept_ref, owner):
    product = jnp.dot(piece, factor, preferred_element_type=F32)
    trailing = (weight_ref[...].astype(F32) - product).astype(BF)
    return jnp.where(owner > 0, kept_ref[...], trailing)


def own_kernel(at_ref, piece_ref, token_ref, *rest):
    parts = rest[:5]
    weight_ref, kept_ref, out_ref, factor_ref = rest[5:]
    for place, part in enumerate(parts):
        start = pl.multiple_of(at_ref[2 + place] * LANE_ROWS, 16)
        factor_ref[pl.ds(start, part.shape[0]), :] = part[...]
    out_ref[...] = subtract(piece_ref[...], factor_ref[...], weight_ref, kept_ref, at_ref[1])


def near_kernel(at_ref, first_ref, second_ref, factor_ref, weight_ref, kept_ref, out_ref):
    for step, piece_ref in enumerate((first_ref, second_ref)):

        @pl.when(pl.program_id(0) == step)
        def _():
            out_ref[...] = subtract(piece_ref[...], factor_ref[...], weight_ref, kept_ref, at_ref[2])


def far_kernel(at_ref, first_ref, second_ref, factor_ref, weight_ref, kept_ref, out_ref, piece_ref):
    for place, half_ref in enumerate((first_ref, second_ref)):
        start = pl.multiple_of(at_ref[2 + place] * HALF, HALF)
        piece_ref[pl.ds(start, HALF), :] = half_ref[...]
    out_ref[...] = subtract(piece_ref[...], factor_ref[...], weight_ref, kept_ref, at_ref[1])


def finish(kernel, steps, at, inputs, weight, kept, extra=None, scratch=()):
    block = pl.BlockSpec((QUARTER, PCOLS), lambda i, at_ref: (at_ref[i], 0))
    vmem = pl.BlockSpec(memory_space=pltpu.VMEM)
    out_shape = [jax.ShapeDtypeStruct((ROWS_DEV, PCOLS), BF)]
    if extra is not None:
        out_shape.append(extra)
    return pl.pallas_call(
        kernel,
        grid_spec=pltpu.PrefetchScalarGridSpec(
            num_scalar_prefetch=1,
            grid=(steps,),
            in_specs=[vmem] * len(inputs) + [block, block],
            out_specs=[block] + [vmem] * (len(out_shape) - 1),
            scratch_shapes=list(scratch),
        ),
        out_shape=out_shape,
        input_output_aliases={len(inputs) + 2: 0},
        compiler_params=pltpu.CompilerParams(vmem_limit_bytes=36 * 2**20),
    )(at, *inputs, weight, kept)


def col_at(x, zh, core):
    return (x % 4) * 8 + (zh % 4) * 2 + core


def row_at(y, zl):
    return (y % 4) * 2 + zl


def vector(value):
    return jnp.reshape(value, (1,)).astype(jnp.int32)


def per_device(weight, factor, keep_mask):
    section = lax.axis_index("col")
    lane = lax.axis_index("row")
    x_at = section // 8
    zh_at = (section // 2) % 4
    core_at = section % 2
    payload, factor_low = local_part(vector(lane), factor)

    def hop(array, dy, flip):
        pairs = [(row_at(y, zl), row_at(y + dy, zl ^ flip)) for y in range(4) for zl in (0, 1)]
        return lax.ppermute(array, ("col", "row"), pairs)

    y_at, zl_at = lane // 2, lane % 2
    up_same = hop(payload, 1, 0)
    down_other = hop(payload, 3, 1)
    up_other = hop(payload, 1, 1)
    down_same = hop(payload, 3, 0)
    other = hop(payload, 0, 1)
    far_same = hop(up_same, 1, 0)
    far_other = hop(down_other, 3, 0)
    pieces = [payload, up_same, down_other, up_other, down_same, other, far_same, far_other]
    order = [
        lane,
        row_at(y_at + 3, zl_at),
        row_at(y_at + 1, 1 - zl_at),
        row_at(y_at + 3, 1 - zl_at),
        row_at(y_at + 1, zl_at),
        row_at(y_at, 1 - zl_at),
        row_at(y_at + 2, zl_at),
        row_at(y_at + 2, 1 - zl_at),
    ]
    *quarters, kept = prune(keep_mask, jnp.stack(order).astype(jnp.int32), weight, pieces)

    def along(array, dy):
        return lax.ppermute(array, "row", [(row_at(y, zl), row_at(y + dy, zl)) for y in range(4) for zl in (0, 1)])

    token = lax.ppermute(factor_low[:16, :BLK], "col", [(0, 1)])
    partner = lax.ppermute(factor_low, "row", [(k, k ^ 1) for k in range(LANES)])
    even = zl_at == 0
    pair = jnp.concatenate(
        [jnp.where(even, factor_low, partner), jnp.where(even, partner, factor_low)], axis=0
    )
    pair_up = along(pair, 1)
    pair_down = along(pair, 3)
    far_even = along(pair_up[:LANE_ROWS], 1)
    far_odd = along(pair_down[LANE_ROWS:], 3)
    parts = (pair, pair_up, pair_down, far_even, far_odd)
    part_rows = [
        row_at(y_at, 0), row_at(y_at + 3, 0), row_at(y_at + 1, 0), row_at(y_at + 2, 0), row_at(y_at + 2, 1)
    ]

    got = None
    for k in (2, 1, 3):
        sent = lax.ppermute(quarters[k], "col", [(0, col_at(k, 0, 0))])
        got = sent if got is None else got + sent
    own = jnp.where(x_at == 0, quarters[0], got)
    up = lax.ppermute(own, "col", [(col_at(x, 0, 0), col_at(x, 1, 0)) for x in range(4)])
    down = lax.ppermute(own, "col", [(col_at(x, 0, 0), col_at(x, 3, 0)) for x in range(4)])
    far_a = lax.ppermute(up[:HALF], "col", [(col_at(x, 1, 0), col_at(x, 2, 0)) for x in range(4)])
    far_b = lax.ppermute(down[HALF:], "col", [(col_at(x, 3, 0), col_at(x, 2, 0)) for x in range(4)])
    own = jnp.where(zh_at == 0, own, up + down + jnp.concatenate([far_a, far_b], axis=0))

    places = [(x, z) for x in range(4) for z in range(4)]
    share = [(col_at(x, z, 0), col_at(x, z, 1)) for x, z in places]
    swap = [(col_at(x, z, c), col_at(x, z, 1 - c)) for x, z in places for c in (0, 1)]
    ring = [(col_at(x, z, 0), col_at(x + 1, z, 0)) for x, z in places]
    ring += [(col_at(x, z, 1), col_at(x - 1, z, 1)) for x, z in places]
    shared = lax.ppermute(own, "col", share)
    own = jnp.where(core_at == 0, own, shared)
    near = lax.ppermute(own, "col", ring)
    far = lax.ppermute(lax.dynamic_slice(near, (core_at * HALF, 0), (HALF, PCOLS)), "col", ring)
    near_other = lax.ppermute(near, "col", swap)
    far_other = lax.ppermute(far, "col", swap)

    def ints(*values):
        return jnp.stack(values).astype(jnp.int32)

    owner = section == 0
    factor_shape = pltpu.VMEM((PCOLS, PCOLS), BF)
    out, factor_all = finish(
        own_kernel, 1, ints(x_at, owner, *part_rows), (own, token, *parts), weight, kept, factor_shape
    )
    ways = ints((x_at + 3 - 2 * core_at) % 4, (x_at + 1 + 2 * core_at) % 4, owner)
    (out,) = finish(near_kernel, 2, ways, (near, near_other, factor_all), weight, out)
    (out,) = finish(
        far_kernel,
        1,
        ints((x_at + 2) % 4, owner, core_at, 1 - core_at),
        (far, far_other, factor_all),
        weight,
        out,
        scratch=[pltpu.VMEM((QUARTER, PCOLS), BF)],
    )
    return out


def solution(mesh):
    in_specs = (P("row", "col"), P("row", "col"), P("row", None))
    out_specs = P("row", "col")
    return jax.shard_map(per_device, mesh=mesh, in_specs=in_specs, out_specs=out_specs, check_vma=False)
```

```python
import jax
import jax.numpy as jnp
from jax import lax
from jax.experimental import pallas as pl
from jax.experimental.pallas import tpu as pltpu
from jax.sharding import PartitionSpec as P


BLK = 128
PCOLS = 1664
LANES = 8
LANE_ROWS = 208
STRIP_BLOCKS = 3
PAD = 256
NBLK = PCOLS // BLK
ROWS_DEV = 1024
QUARTER = 256
FORWARD = 64
BF = jnp.bfloat16
F32 = jnp.float32


def split(a):
    high = a.astype(BF)
    return high, (a - high.astype(F32)).astype(BF)


def mm_split(a, b):
    right = jnp.concatenate(split(b), axis=1)
    left = jnp.concatenate(split(a), axis=1)
    both = jnp.dot(left, jnp.concatenate([right, right], axis=0), preferred_element_type=F32)
    return both[:, :BLK] + both[:, BLK:]


def triangle_inverses(fulls):
    row = lax.broadcasted_iota(jnp.int32, (BLK, BLK), 0)
    column = lax.broadcasted_iota(jnp.int32, (BLK, BLK), 1)
    eye = (row == column).astype(F32)
    stricts, pivots = [], []
    for full in fulls:
        on_diag = jnp.where(row == column, full, 0.0)
        pivots.append(jnp.sum(on_diag, axis=0, keepdims=True))
        stricts.append(jnp.where(column > row, full, 0.0) / jnp.sum(on_diag, axis=1, keepdims=True))
    nears = [jnp.where((row // 8) == (column // 8), strict, 0.0) for strict in stricts]
    near2s = [mm_split(near, near) for near in nears]
    near4s = [mm_split(near2, near2) for near2 in near2s]
    inverses = [mm_split(eye - near, eye + near2) for near, near2 in zip(nears, near2s)]
    inverses = [mm_split(inverse, eye + near4) for inverse, near4 in zip(inverses, near4s)]
    width = 8
    while width < BLK:
        pair = 2 * width
        inside = ((row // pair) == (column // pair)) & ((row // width) != (column // width))
        offs = [jnp.where(inside, strict, 0.0) for strict in stricts]
        steps = [mm_split(off, inverse) for off, inverse in zip(offs, inverses)]
        inverses = [inverse - mm_split(inverse, step) for inverse, step in zip(inverses, steps)]
        width = pair
    return [inverse / pivot for inverse, pivot in zip(inverses, pivots)]


def local_kernel(lane_ref, factor_ref, payload_ref, low_ref, rows_ref, inverse_ref):
    lane = lane_ref[0]
    first = jnp.minimum(lane * LANE_ROWS // BLK, NBLK - STRIP_BLOCKS)
    low = factor_ref[...].astype(BF)
    payload_ref[:, :PCOLS] = low
    low_ref[...] = low
    start = pl.multiple_of(first * BLK, BLK)
    rows_ref[PAD : PAD + LANE_ROWS, :] = factor_ref[:, pl.ds(start, STRIP_BLOCKS * BLK)]
    row = lax.broadcasted_iota(jnp.int32, (BLK, BLK), 0)
    column = lax.broadcasted_iota(jnp.int32, (BLK, BLK), 1)
    eye = (row == column).astype(F32)
    fulls, places = [], []
    for place in range(STRIP_BLOCKS):
        shift = (first + place) * BLK - lane * LANE_ROWS
        at = pl.multiple_of(shift + PAD, 16)
        valid = (row + shift >= 0) & (row + shift < LANE_ROWS)
        block = rows_ref[pl.ds(at, BLK), place * BLK : (place + 1) * BLK]
        fulls.append(jnp.where(valid, block, eye))
        places.append((at, valid))
    for (at, valid), inverse in zip(places, triangle_inverses(fulls)):
        here = inverse_ref[pl.ds(at, BLK), :]
        inverse_ref[pl.ds(at, BLK), :] = jnp.where(valid, inverse, here)
    high, lowpart = split(inverse_ref[PAD : PAD + LANE_ROWS, :])
    payload_ref[:, PCOLS : PCOLS + BLK] = high
    payload_ref[:, PCOLS + BLK :] = lowpart


def local_part(lane, factor):
    vmem = pl.BlockSpec(memory_space=pltpu.VMEM)
    smem = pl.BlockSpec(memory_space=pltpu.SMEM)
    return pl.pallas_call(
        local_kernel,
        in_specs=[smem, vmem],
        out_specs=(vmem, vmem),
        out_shape=(
            jax.ShapeDtypeStruct((LANE_ROWS, PCOLS + 2 * BLK), BF),
            jax.ShapeDtypeStruct((LANE_ROWS, PCOLS), BF),
        ),
        scratch_shapes=[
            pltpu.VMEM((PAD + LANE_ROWS + PAD, STRIP_BLOCKS * BLK), F32),
            pltpu.VMEM((PAD + LANE_ROWS + PAD, BLK), F32),
        ],
        name="local_part",
    )(lane, factor)


def prune_kernel(keep_ref, order_ref, weight_hbm, *rest):
    pieces = rest[:LANES]
    part_refs = rest[LANES : 2 * LANES]
    kept_ref, factor_ref, errors_ref, weight_ref, sems = rest[2 * LANES :]
    copies = [pltpu.make_async_copy(weight_hbm, weight_ref, sems.at[LANES])]
    for place in range(LANES):
        start = pl.multiple_of(order_ref[place] * LANE_ROWS, 16)
        copies.append(
            pltpu.make_async_copy(pieces[place], factor_ref.at[pl.ds(start, LANE_ROWS), :], sems.at[place])
        )
    for copy in copies:
        copy.start()
    for copy in copies:
        copy.wait()
    row = lax.broadcasted_iota(jnp.int32, (BLK, BLK), 0)
    column = lax.broadcasted_iota(jnp.int32, (BLK, BLK), 1)
    eye = (row == column).astype(F32)
    for block in range(NBLK):
        at = block * BLK
        edge = (at // LANE_ROWS + 1) * LANE_ROWS - at
        if edge < BLK:
            stored = factor_ref[at : at + BLK, PCOLS:]
            whole = stored[:, :BLK].astype(F32) + stored[:, BLK:].astype(F32)
            top = jnp.where(row < edge, whole, eye)
            bottom = jnp.where(row < edge, eye, whole)
            factor_ref[at : at + BLK, PCOLS:] = jnp.concatenate(split(mm_split(top, bottom)), axis=1)
    for low in range(0, PCOLS, 2 * BLK):
        width = min(2 * BLK, PCOLS - low)
        current = weight_ref[:, low : low + width].astype(F32)
        if low:
            current = current - jnp.dot(
                errors_ref[:, :low], factor_ref[:low, low : low + width], preferred_element_type=F32
            )
        for half in range(width // BLK):
            at = low + half * BLK
            part = current[:, half * BLK : (half + 1) * BLK]
            if half:
                part = part - jnp.dot(
                    errors_ref[:, low : low + BLK],
                    factor_ref[low : low + BLK, at : at + BLK],
                    preferred_element_type=F32,
                )
            high, lowpart = split(part)
            right = factor_ref[at : at + BLK, PCOLS:]
            both = jnp.dot(
                jnp.concatenate([high, lowpart], axis=1),
                jnp.concatenate([right, right], axis=0),
                preferred_element_type=F32,
            )
            solved = (both[:, :BLK] + both[:, BLK:]).astype(BF)
            for group in range(ROWS_DEV // BLK):
                top = group * BLK
                keep = keep_ref[group, at // BLK] > 0
                error = jnp.where(keep, jnp.zeros((BLK, BLK), BF), solved[top : top + BLK])
                errors_ref[top : top + BLK, at : at + BLK] = error
                part_refs[group][:, at : at + BLK] = error
                kept_ref[top : top + BLK, at : at + BLK] = jnp.where(
                    keep, high[top : top + BLK], jnp.zeros((BLK, BLK), BF)
                )


def prune(keep_mask, order, weight, pieces):
    vmem = pl.BlockSpec(memory_space=pltpu.VMEM)
    smem = pl.BlockSpec(memory_space=pltpu.SMEM)
    hbm = pl.BlockSpec(memory_space=pl.ANY)
    part = jax.ShapeDtypeStruct((BLK, PCOLS), BF)
    return pl.pallas_call(
        prune_kernel,
        in_specs=[smem, smem, hbm] + [hbm] * LANES,
        out_specs=(vmem,) * (LANES + 1),
        out_shape=(part,) * LANES + (jax.ShapeDtypeStruct((ROWS_DEV, PCOLS), BF),),
        scratch_shapes=[
            pltpu.VMEM((PCOLS, PCOLS + 2 * BLK), BF),
            pltpu.VMEM((ROWS_DEV, PCOLS), BF),
            pltpu.VMEM((ROWS_DEV, PCOLS), BF),
            pltpu.SemaphoreType.DMA((LANES + 1,)),
        ],
        name="prune",
    )(keep_mask, order, weight, *pieces)


def subtract(piece, factor, weight_ref, kept_ref, owner):
    product = jnp.dot(piece, factor, preferred_element_type=F32)
    trailing = (weight_ref[...].astype(F32) - product).astype(BF)
    return jnp.where(owner > 0, kept_ref[...], trailing)


def own_kernel(at_ref, first_ref, second_ref, token_ref, *rest):
    parts = rest[:5]
    weight_ref, kept_ref, out_ref, factor_ref = rest[5:]
    for place, part in enumerate(parts):
        start = pl.multiple_of(at_ref[2 + place] * LANE_ROWS, 16)
        factor_ref[pl.ds(start, part.shape[0]), :] = part[...]
    piece = jnp.concatenate([first_ref[...], second_ref[...]], axis=0)
    out_ref[...] = subtract(piece, factor_ref[...], weight_ref, kept_ref, at_ref[1])


def near_kernel(at_ref, *rest):
    pieces = rest[:4]
    factor_ref, weight_ref, kept_ref, out_ref = rest[4:]
    for step in range(2):

        @pl.when(pl.program_id(0) == step)
        def _():
            piece = jnp.concatenate([pieces[2 * step][...], pieces[2 * step + 1][...]], axis=0)
            out_ref[...] = subtract(piece, factor_ref[...], weight_ref, kept_ref, at_ref[2])


def far_kernel(at_ref, *rest):
    pieces = rest[:4]
    factor_ref, weight_ref, kept_ref, out_ref, piece_ref = rest[4:]
    for place, part_ref in enumerate(pieces):
        start = pl.multiple_of(at_ref[2 + place] * FORWARD, FORWARD)
        piece_ref[pl.ds(start, FORWARD), :] = part_ref[...]
    out_ref[...] = subtract(piece_ref[...], factor_ref[...], weight_ref, kept_ref, at_ref[1])


def finish(kernel, steps, at, inputs, weight, kept, extra=None, scratch=()):
    block = pl.BlockSpec((QUARTER, PCOLS), lambda i, at_ref: (at_ref[i], 0))
    vmem = pl.BlockSpec(memory_space=pltpu.VMEM)
    out_shape = [jax.ShapeDtypeStruct((ROWS_DEV, PCOLS), BF)]
    if extra is not None:
        out_shape.append(extra)
    return pl.pallas_call(
        kernel,
        grid_spec=pltpu.PrefetchScalarGridSpec(
            num_scalar_prefetch=1,
            grid=(steps,),
            in_specs=[vmem] * len(inputs) + [block, block],
            out_specs=[block] + [vmem] * (len(out_shape) - 1),
            scratch_shapes=list(scratch),
        ),
        out_shape=out_shape,
        input_output_aliases={len(inputs) + 2: 0},
    )(at, *inputs, weight, kept)


def col_at(x, zh, core):
    return (x % 4) * 8 + (zh % 4) * 2 + core


def row_at(y, zl):
    return (y % 4) * 2 + zl


def vector(value):
    return jnp.reshape(value, (1,)).astype(jnp.int32)


def per_device(weight, factor, keep_mask):
    section = lax.axis_index("col")
    lane = lax.axis_index("row")
    x_at = section // 8
    zh_at = (section // 2) % 4
    core_at = section % 2
    payload, factor_low = local_part(vector(lane), factor)

    def hop(array, dy, flip):
        pairs = [(row_at(y, zl), row_at(y + dy, zl ^ flip)) for y in range(4) for zl in (0, 1)]
        return lax.ppermute(array, ("col", "row"), pairs)

    y_at, zl_at = lane // 2, lane % 2
    up_same = hop(payload, 1, 0)
    down_other = hop(payload, 3, 1)
    up_other = hop(payload, 1, 1)
    down_same = hop(payload, 3, 0)
    other = hop(payload, 0, 1)
    far_same = hop(up_same, 1, 0)
    far_other = hop(down_other, 3, 0)
    pieces = [payload, up_same, down_other, up_other, down_same, other, far_same, far_other]
    order = [
        lane,
        row_at(y_at + 3, zl_at),
        row_at(y_at + 1, 1 - zl_at),
        row_at(y_at + 3, 1 - zl_at),
        row_at(y_at + 1, zl_at),
        row_at(y_at, 1 - zl_at),
        row_at(y_at + 2, zl_at),
        row_at(y_at + 2, 1 - zl_at),
    ]
    *parts_out, kept = prune(keep_mask, jnp.stack(order).astype(jnp.int32), weight, pieces)

    def along(array, dy):
        return lax.ppermute(array, "row", [(row_at(y, zl), row_at(y + dy, zl)) for y in range(4) for zl in (0, 1)])

    token = lax.ppermute(factor_low[:16, :BLK], "col", [(0, 1)])
    partner = lax.ppermute(factor_low, "row", [(k, k ^ 1) for k in range(LANES)])
    even = zl_at == 0
    pair = jnp.concatenate(
        [jnp.where(even, factor_low, partner), jnp.where(even, partner, factor_low)], axis=0
    )
    pair_up = along(pair, 1)
    pair_down = along(pair, 3)
    far_even = along(pair_up[:LANE_ROWS], 1)
    far_odd = along(pair_down[LANE_ROWS:], 3)
    parts = (pair, pair_up, pair_down, far_even, far_odd)
    part_rows = [
        row_at(y_at, 0), row_at(y_at + 3, 0), row_at(y_at + 1, 0), row_at(y_at + 2, 0), row_at(y_at + 2, 1)
    ]

    places = [(x, z) for x in range(4) for z in range(4)]
    share = [(col_at(x, z, 0), col_at(x, z, 1)) for x, z in places]
    swap = [(col_at(x, z, c), col_at(x, z, 1 - c)) for x, z in places for c in (0, 1)]
    ring = [(col_at(x, z, 0), col_at(x + 1, z, 0)) for x, z in places]
    ring += [(col_at(x, z, 1), col_at(x - 1, z, 1)) for x, z in places]
    owns, nears, near_others, fars, far_others = [], [], [], [], []
    for chunk in (0, 1):
        got = None
        for k in (2, 1, 3):
            sent = lax.ppermute(parts_out[2 * k + chunk], "col", [(0, col_at(k, 0, 0))])
            got = sent if got is None else got + sent
        own = jnp.where(x_at == 0, parts_out[chunk], got)
        up = lax.ppermute(own, "col", [(col_at(x, 0, 0), col_at(x, 1, 0)) for x in range(4)])
        down = lax.ppermute(own, "col", [(col_at(x, 0, 0), col_at(x, 3, 0)) for x in range(4)])
        far_a = lax.ppermute(up[:FORWARD], "col", [(col_at(x, 1, 0), col_at(x, 2, 0)) for x in range(4)])
        far_b = lax.ppermute(down[FORWARD:], "col", [(col_at(x, 3, 0), col_at(x, 2, 0)) for x in range(4)])
        own = jnp.where(zh_at == 0, own, up + down + jnp.concatenate([far_a, far_b], axis=0))

        shared = lax.ppermute(own, "col", share)
        own = jnp.where(core_at == 0, own, shared)
        near = lax.ppermute(own, "col", ring)
        onward = lax.dynamic_slice(near, (core_at * FORWARD, 0), (FORWARD, PCOLS))
        far = lax.ppermute(onward, "col", ring)
        owns.append(own)
        nears.append(near)
        fars.append(far)
        near_others.append(lax.ppermute(near, "col", swap))
        far_others.append(lax.ppermute(far, "col", swap))

    def ints(*values):
        return jnp.stack([jnp.asarray(value) for value in values]).astype(jnp.int32)

    owner = section == 0
    factor_shape = jax.ShapeDtypeStruct((PCOLS, PCOLS), BF)
    out, factor_all = finish(
        own_kernel, 1, ints(x_at, owner, *part_rows), (*owns, token, *parts), weight, kept, factor_shape
    )
    ways = ints((x_at + 3 - 2 * core_at) % 4, (x_at + 1 + 2 * core_at) % 4, owner)
    (out,) = finish(near_kernel, 2, ways, (*nears, *near_others, factor_all), weight, out)
    (out,) = finish(
        far_kernel,
        1,
        ints((x_at + 2) % 4, owner, core_at, 2 + core_at, 1 - core_at, 3 - core_at),
        (*fars, *far_others, factor_all),
        weight,
        out,
        scratch=[pltpu.VMEM((QUARTER, PCOLS), BF)],
    )
    return out


def solution(mesh):
    in_specs = (P("row", "col"), P("row", "col"), P("row", None))
    out_specs = P("row", "col")
    return jax.shard_map(per_device, mesh=mesh, in_specs=in_specs, out_specs=out_specs, check_vma=False)
```

```python
import jax
import jax.numpy as jnp
from jax import lax
from jax.experimental import pallas as pl
from jax.experimental.pallas import tpu as pltpu
from jax.sharding import PartitionSpec as P


BLK = 128
PCOLS = 1664
LANES = 8
LANE_ROWS = 208
STRIP_BLOCKS = 3
PAD = 256
NBLK = PCOLS // BLK
ROWS_DEV = 1024
QUARTER = 256
FORWARD = 64
BF = jnp.bfloat16
F32 = jnp.float32


def split(a):
    high = a.astype(BF)
    return high, (a - high.astype(F32)).astype(BF)


def mm_split(a, b):
    right = jnp.concatenate(split(b), axis=1)
    left = jnp.concatenate(split(a), axis=1)
    both = jnp.dot(left, jnp.concatenate([right, right], axis=0), preferred_element_type=F32)
    return both[:, :BLK] + both[:, BLK:]


def triangle_inverses(fulls):
    row = lax.broadcasted_iota(jnp.int32, (BLK, BLK), 0)
    column = lax.broadcasted_iota(jnp.int32, (BLK, BLK), 1)
    eye = (row == column).astype(F32)
    stricts, pivots = [], []
    for full in fulls:
        on_diag = jnp.where(row == column, full, 0.0)
        pivots.append(jnp.sum(on_diag, axis=0, keepdims=True))
        stricts.append(jnp.where(column > row, full, 0.0) / jnp.sum(on_diag, axis=1, keepdims=True))
    nears = [jnp.where((row // 8) == (column // 8), strict, 0.0) for strict in stricts]
    near2s = [mm_split(near, near) for near in nears]
    near4s = [mm_split(near2, near2) for near2 in near2s]
    inverses = [mm_split(eye - near, eye + near2) for near, near2 in zip(nears, near2s)]
    inverses = [mm_split(inverse, eye + near4) for inverse, near4 in zip(inverses, near4s)]
    width = 8
    while width < BLK:
        pair = 2 * width
        inside = ((row // pair) == (column // pair)) & ((row // width) != (column // width))
        offs = [jnp.where(inside, strict, 0.0) for strict in stricts]
        steps = [mm_split(off, inverse) for off, inverse in zip(offs, inverses)]
        inverses = [inverse - mm_split(inverse, step) for inverse, step in zip(inverses, steps)]
        width = pair
    return [inverse / pivot for inverse, pivot in zip(inverses, pivots)]


def local_kernel(lane_ref, factor_ref, payload_ref, low_ref, rows_ref, inverse_ref):
    lane = lane_ref[0]
    first = jnp.minimum(lane * LANE_ROWS // BLK, NBLK - STRIP_BLOCKS)
    low = factor_ref[...].astype(BF)
    payload_ref[:, :PCOLS] = low
    low_ref[...] = low
    start = pl.multiple_of(first * BLK, BLK)
    rows_ref[PAD : PAD + LANE_ROWS, :] = factor_ref[:, pl.ds(start, STRIP_BLOCKS * BLK)]
    row = lax.broadcasted_iota(jnp.int32, (BLK, BLK), 0)
    column = lax.broadcasted_iota(jnp.int32, (BLK, BLK), 1)
    eye = (row == column).astype(F32)
    fulls, places = [], []
    for place in range(STRIP_BLOCKS):
        shift = (first + place) * BLK - lane * LANE_ROWS
        at = pl.multiple_of(shift + PAD, 16)
        valid = (row + shift >= 0) & (row + shift < LANE_ROWS)
        block = rows_ref[pl.ds(at, BLK), place * BLK : (place + 1) * BLK]
        fulls.append(jnp.where(valid, block, eye))
        places.append((at, valid))
    for (at, valid), inverse in zip(places, triangle_inverses(fulls)):
        here = inverse_ref[pl.ds(at, BLK), :]
        inverse_ref[pl.ds(at, BLK), :] = jnp.where(valid, inverse, here)
    high, lowpart = split(inverse_ref[PAD : PAD + LANE_ROWS, :])
    payload_ref[:, PCOLS : PCOLS + BLK] = high
    payload_ref[:, PCOLS + BLK :] = lowpart


def local_part(lane, factor):
    vmem = pl.BlockSpec(memory_space=pltpu.VMEM)
    smem = pl.BlockSpec(memory_space=pltpu.SMEM)
    return pl.pallas_call(
        local_kernel,
        in_specs=[smem, vmem],
        out_specs=(vmem, vmem),
        out_shape=(
            jax.ShapeDtypeStruct((LANE_ROWS, PCOLS + 2 * BLK), BF),
            jax.ShapeDtypeStruct((LANE_ROWS, PCOLS), BF),
        ),
        scratch_shapes=[
            pltpu.VMEM((PAD + LANE_ROWS + PAD, STRIP_BLOCKS * BLK), F32),
            pltpu.VMEM((PAD + LANE_ROWS + PAD, BLK), F32),
        ],
        name="local_part",
    )(lane, factor)


def prune_kernel(keep_ref, order_ref, weight_hbm, *rest):
    pieces = rest[:LANES]
    part_refs = rest[LANES : 2 * LANES]
    kept_ref, factor_ref, errors_ref, weight_ref, sems = rest[2 * LANES :]
    copies = [pltpu.make_async_copy(weight_hbm, weight_ref, sems.at[LANES])]
    for place in range(LANES):
        start = pl.multiple_of(order_ref[place] * LANE_ROWS, 16)
        copies.append(
            pltpu.make_async_copy(pieces[place], factor_ref.at[pl.ds(start, LANE_ROWS), :], sems.at[place])
        )
    for copy in copies:
        copy.start()
    for copy in copies:
        copy.wait()
    row = lax.broadcasted_iota(jnp.int32, (BLK, BLK), 0)
    column = lax.broadcasted_iota(jnp.int32, (BLK, BLK), 1)
    eye = (row == column).astype(F32)
    for block in range(NBLK):
        at = block * BLK
        edge = (at // LANE_ROWS + 1) * LANE_ROWS - at
        if edge < BLK:
            stored = factor_ref[at : at + BLK, PCOLS:]
            whole = stored[:, :BLK].astype(F32) + stored[:, BLK:].astype(F32)
            top = jnp.where(row < edge, whole, eye)
            bottom = jnp.where(row < edge, eye, whole)
            factor_ref[at : at + BLK, PCOLS:] = jnp.concatenate(split(mm_split(top, bottom)), axis=1)
    for low in range(0, PCOLS, 2 * BLK):
        width = min(2 * BLK, PCOLS - low)
        current = weight_ref[:, low : low + width].astype(F32)
        if low:
            current = current - jnp.dot(
                errors_ref[:, :low], factor_ref[:low, low : low + width], preferred_element_type=F32
            )
        for half in range(width // BLK):
            at = low + half * BLK
            part = current[:, half * BLK : (half + 1) * BLK]
            if half:
                part = part - jnp.dot(
                    errors_ref[:, low : low + BLK],
                    factor_ref[low : low + BLK, at : at + BLK],
                    preferred_element_type=F32,
                )
            high, lowpart = split(part)
            right = factor_ref[at : at + BLK, PCOLS:]
            both = jnp.dot(
                jnp.concatenate([high, lowpart], axis=1),
                jnp.concatenate([right, right], axis=0),
                preferred_element_type=F32,
            )
            solved = (both[:, :BLK] + both[:, BLK:]).astype(BF)
            for group in range(ROWS_DEV // BLK):
                top = group * BLK
                keep = keep_ref[group, at // BLK] > 0
                error = jnp.where(keep, jnp.zeros((BLK, BLK), BF), solved[top : top + BLK])
                errors_ref[top : top + BLK, at : at + BLK] = error
                part_refs[group][:, at : at + BLK] = error
                kept_ref[top : top + BLK, at : at + BLK] = jnp.where(
                    keep, high[top : top + BLK], jnp.zeros((BLK, BLK), BF)
                )


def prune(keep_mask, order, weight, pieces):
    vmem = pl.BlockSpec(memory_space=pltpu.VMEM)
    smem = pl.BlockSpec(memory_space=pltpu.SMEM)
    hbm = pl.BlockSpec(memory_space=pl.ANY)
    part = jax.ShapeDtypeStruct((BLK, PCOLS), BF)
    return pl.pallas_call(
        prune_kernel,
        in_specs=[smem, smem, hbm] + [hbm] * LANES,
        out_specs=(vmem,) * (LANES + 1),
        out_shape=(part,) * LANES + (jax.ShapeDtypeStruct((ROWS_DEV, PCOLS), BF),),
        scratch_shapes=[
            pltpu.VMEM((PCOLS, PCOLS + 2 * BLK), BF),
            pltpu.VMEM((ROWS_DEV, PCOLS), BF),
            pltpu.VMEM((ROWS_DEV, PCOLS), BF),
            pltpu.SemaphoreType.DMA((LANES + 1,)),
        ],
        name="prune",
    )(keep_mask, order, weight, *pieces)


def subtract(piece, factor, weight_ref, kept_ref, owner):
    product = jnp.dot(piece, factor, preferred_element_type=F32)
    trailing = (weight_ref[...].astype(F32) - product).astype(BF)
    return jnp.where(owner > 0, kept_ref[...], trailing)


def own_kernel(at_ref, first_ref, second_ref, token_ref, *rest):
    parts = rest[:LANES]
    weight_ref, kept_ref, out_ref, factor_ref = rest[LANES:]
    for place, part in enumerate(parts):
        start = pl.multiple_of(at_ref[2 + place] * LANE_ROWS, 16)
        factor_ref[pl.ds(start, part.shape[0]), :] = part[...]
    piece = jnp.concatenate([first_ref[...], second_ref[...]], axis=0)
    out_ref[...] = subtract(piece, factor_ref[...], weight_ref, kept_ref, at_ref[1])


def near_kernel(at_ref, *rest):
    pieces = rest[:4]
    factor_ref, weight_ref, kept_ref, out_ref = rest[4:]
    for step in range(2):

        @pl.when(pl.program_id(0) == step)
        def _():
            piece = jnp.concatenate([pieces[2 * step][...], pieces[2 * step + 1][...]], axis=0)
            out_ref[...] = subtract(piece, factor_ref[...], weight_ref, kept_ref, at_ref[2])


def far_kernel(at_ref, *rest):
    pieces = rest[:4]
    factor_ref, weight_ref, kept_ref, out_ref, piece_ref = rest[4:]
    for place, part_ref in enumerate(pieces):
        start = pl.multiple_of(at_ref[2 + place] * FORWARD, FORWARD)
        piece_ref[pl.ds(start, FORWARD), :] = part_ref[...]
    out_ref[...] = subtract(piece_ref[...], factor_ref[...], weight_ref, kept_ref, at_ref[1])


def finish(kernel, steps, at, inputs, weight, kept, extra=None, scratch=()):
    block = pl.BlockSpec((QUARTER, PCOLS), lambda i, at_ref: (at_ref[i], 0))
    vmem = pl.BlockSpec(memory_space=pltpu.VMEM)
    out_shape = [jax.ShapeDtypeStruct((ROWS_DEV, PCOLS), BF)]
    if extra is not None:
        out_shape.append(extra)
    return pl.pallas_call(
        kernel,
        grid_spec=pltpu.PrefetchScalarGridSpec(
            num_scalar_prefetch=1,
            grid=(steps,),
            in_specs=[vmem] * len(inputs) + [block, block],
            out_specs=[block] + [vmem] * (len(out_shape) - 1),
            scratch_shapes=list(scratch),
        ),
        out_shape=out_shape,
        input_output_aliases={len(inputs) + 2: 0},
    )(at, *inputs, weight, kept)


def col_at(x, zh, core):
    return (x % 4) * 8 + (zh % 4) * 2 + core


def row_at(y, zl):
    return (y % 4) * 2 + zl


def vector(value):
    return jnp.reshape(value, (1,)).astype(jnp.int32)


def per_device(weight, factor, keep_mask):
    section = lax.axis_index("col")
    lane = lax.axis_index("row")
    x_at = section // 8
    zh_at = (section // 2) % 4
    core_at = section % 2
    payload, factor_low = local_part(vector(lane), factor)

    def hop(array, dy, flip):
        pairs = [(row_at(y, zl), row_at(y + dy, zl ^ flip)) for y in range(4) for zl in (0, 1)]
        return lax.ppermute(array, ("col", "row"), pairs)

    y_at, zl_at = lane // 2, lane % 2
    up_same = hop(payload, 1, 0)
    down_other = hop(payload, 3, 1)
    up_other = hop(payload, 1, 1)
    down_same = hop(payload, 3, 0)
    other = hop(payload, 0, 1)
    far_same = hop(up_same, 1, 0)
    far_other = hop(down_other, 3, 0)
    pieces = [payload, up_same, down_other, up_other, down_same, other, far_same, far_other]
    order = [
        lane,
        row_at(y_at + 3, zl_at),
        row_at(y_at + 1, 1 - zl_at),
        row_at(y_at + 3, 1 - zl_at),
        row_at(y_at + 1, zl_at),
        row_at(y_at, 1 - zl_at),
        row_at(y_at + 2, zl_at),
        row_at(y_at + 2, 1 - zl_at),
    ]
    *parts_out, kept = prune(keep_mask, jnp.stack(order).astype(jnp.int32), weight, pieces)

    def along(array, dy, flip=0):
        pairs = [
            (c * LANES + row_at(y, zl), c * LANES + row_at(y + dy, zl ^ flip))
            for c in range(1, 32)
            for y in range(4)
            for zl in (0, 1)
        ]
        return lax.ppermute(array, ("col", "row"), pairs)

    token = lax.ppermute(factor_low[:16, :BLK], "col", [(0, 1)])
    partner = along(factor_low, 0, 1)
    even = jnp.where(zl_at == 0, factor_low, partner)
    odd = jnp.where(zl_at == 0, partner, factor_low)
    even_up = along(even, 1)
    odd_down = along(odd, 3)
    odd_up = along(odd, 1)
    even_down = along(even, 3)
    even_far = along(even_up, 1)
    odd_far = along(odd_down, 3)
    parts = (even, odd, even_up, odd_up, even_down, odd_down, even_far, odd_far)
    part_rows = [row_at(y_at + dy, zl) for dy in (0, 3, 1, 2) for zl in (0, 1)]

    places = [(x, z) for x in range(4) for z in range(4)]
    share = [(col_at(x, z, 0), col_at(x, z, 1)) for x, z in places]
    swap = [(col_at(x, z, c), col_at(x, z, 1 - c)) for x, z in places for c in (0, 1)]
    ring = [(col_at(x, z, 0), col_at(x + 1, z, 0)) for x, z in places]
    ring += [(col_at(x, z, 1), col_at(x - 1, z, 1)) for x, z in places]
    owns, nears, near_others, fars, far_others = [], [], [], [], []
    for chunk in (0, 1):
        got = None
        for k in (2, 1, 3):
            sent = lax.ppermute(parts_out[2 * k + chunk], "col", [(0, col_at(k, 0, 0))])
            got = sent if got is None else got + sent
        own = jnp.where(x_at == 0, parts_out[chunk], got)
        up = lax.ppermute(own, "col", [(col_at(x, 0, 0), col_at(x, 1, 0)) for x in range(4)])
        down = lax.ppermute(own, "col", [(col_at(x, 0, 0), col_at(x, 3, 0)) for x in range(4)])
        side, array = ((1, up), (3, down))[chunk]
        far_z = lax.ppermute(array, "col", [(col_at(x, side, 0), col_at(x, 2, 0)) for x in range(4)])
        own = jnp.where(zh_at == 0, own, up + down + far_z)

        shared = lax.ppermute(own, "col", share)
        own = jnp.where(core_at == 0, own, shared)
        near = lax.ppermute(own, "col", ring)
        onward = lax.dynamic_slice(near, (core_at * FORWARD, 0), (FORWARD, PCOLS))
        far = lax.ppermute(onward, "col", ring)
        owns.append(own)
        nears.append(near)
        fars.append(far)
        near_others.append(lax.ppermute(near, "col", swap))
        far_others.append(lax.ppermute(far, "col", swap))

    def ints(*values):
        return jnp.stack([jnp.asarray(value) for value in values]).astype(jnp.int32)

    owner = section == 0
    factor_shape = jax.ShapeDtypeStruct((PCOLS, PCOLS), BF)
    out, factor_all = finish(
        own_kernel, 1, ints(x_at, owner, *part_rows), (*owns, token, *parts), weight, kept, factor_shape
    )
    ways = ints((x_at + 3 - 2 * core_at) % 4, (x_at + 1 + 2 * core_at) % 4, owner)
    (out,) = finish(near_kernel, 2, ways, (*nears, *near_others, factor_all), weight, out)
    (out,) = finish(
        far_kernel,
        1,
        ints((x_at + 2) % 4, owner, core_at, 2 + core_at, 1 - core_at, 3 - core_at),
        (*fars, *far_others, factor_all),
        weight,
        out,
        scratch=[pltpu.VMEM((QUARTER, PCOLS), BF)],
    )
    return out


def solution(mesh):
    in_specs = (P("row", "col"), P("row", "col"), P("row", None))
    out_specs = P("row", "col")
    return jax.shard_map(
        per_device, mesh=mesh, in_specs=in_specs, out_specs=out_specs, check_vma=False
    )
```

```python
import jax
import jax.numpy as jnp
from jax import lax
from jax.experimental import pallas as pl
from jax.experimental.pallas import tpu as pltpu
from jax.sharding import PartitionSpec as P


BLK = 128
PCOLS = 1664
LANES = 8
LANE_ROWS = 208
STRIP_BLOCKS = 3
PAD = 256
NBLK = PCOLS // BLK
ROWS_DEV = 1024
QUARTER = 256
FORWARD = 64
SLABS = ((0, 512), (512, 1024), (1024, PCOLS))
BF = jnp.bfloat16
F32 = jnp.float32


def split(a):
    high = a.astype(BF)
    return high, (a - high.astype(F32)).astype(BF)


def mm_split(a, b):
    right = jnp.concatenate(split(b), axis=1)
    left = jnp.concatenate(split(a), axis=1)
    both = jnp.dot(left, jnp.concatenate([right, right], axis=0), preferred_element_type=F32)
    return both[:, :BLK] + both[:, BLK:]


def triangle_inverses(fulls):
    row = lax.broadcasted_iota(jnp.int32, (BLK, BLK), 0)
    column = lax.broadcasted_iota(jnp.int32, (BLK, BLK), 1)
    eye = (row == column).astype(F32)
    stricts, pivots = [], []
    for full in fulls:
        on_diag = jnp.where(row == column, full, 0.0)
        pivots.append(jnp.sum(on_diag, axis=0, keepdims=True))
        stricts.append(jnp.where(column > row, full, 0.0) / jnp.sum(on_diag, axis=1, keepdims=True))
    nears = [jnp.where((row // 8) == (column // 8), strict, 0.0) for strict in stricts]
    near2s = [mm_split(near, near) for near in nears]
    near4s = [mm_split(near2, near2) for near2 in near2s]
    inverses = [mm_split(eye - near, eye + near2) for near, near2 in zip(nears, near2s)]
    inverses = [mm_split(inverse, eye + near4) for inverse, near4 in zip(inverses, near4s)]
    width = 8
    while width < BLK:
        pair = 2 * width
        inside = ((row // pair) == (column // pair)) & ((row // width) != (column // width))
        offs = [jnp.where(inside, strict, 0.0) for strict in stricts]
        steps = [mm_split(off, inverse) for off, inverse in zip(offs, inverses)]
        inverses = [inverse - mm_split(inverse, step) for inverse, step in zip(inverses, steps)]
        width = pair
    return [inverse / pivot for inverse, pivot in zip(inverses, pivots)]


def local_kernel(lane_ref, factor_ref, payload_ref, low_ref, rows_ref, inverse_ref):
    lane = lane_ref[0]
    first = jnp.minimum(lane * LANE_ROWS // BLK, NBLK - STRIP_BLOCKS)
    low = factor_ref[...].astype(BF)
    payload_ref[:, :PCOLS] = low
    low_ref[...] = low
    start = pl.multiple_of(first * BLK, BLK)
    rows_ref[PAD : PAD + LANE_ROWS, :] = factor_ref[:, pl.ds(start, STRIP_BLOCKS * BLK)]
    row = lax.broadcasted_iota(jnp.int32, (BLK, BLK), 0)
    column = lax.broadcasted_iota(jnp.int32, (BLK, BLK), 1)
    eye = (row == column).astype(F32)
    fulls, places = [], []
    for place in range(STRIP_BLOCKS):
        shift = (first + place) * BLK - lane * LANE_ROWS
        at = pl.multiple_of(shift + PAD, 16)
        valid = (row + shift >= 0) & (row + shift < LANE_ROWS)
        block = rows_ref[pl.ds(at, BLK), place * BLK : (place + 1) * BLK]
        fulls.append(jnp.where(valid, block, eye))
        places.append((at, valid))
    for (at, valid), inverse in zip(places, triangle_inverses(fulls)):
        here = inverse_ref[pl.ds(at, BLK), :]
        inverse_ref[pl.ds(at, BLK), :] = jnp.where(valid, inverse, here)
    high, lowpart = split(inverse_ref[PAD : PAD + LANE_ROWS, :])
    payload_ref[:, PCOLS : PCOLS + BLK] = high
    payload_ref[:, PCOLS + BLK :] = lowpart


def local_part(lane, factor):
    vmem = pl.BlockSpec(memory_space=pltpu.VMEM)
    smem = pl.BlockSpec(memory_space=pltpu.SMEM)
    return pl.pallas_call(
        local_kernel,
        in_specs=[smem, vmem],
        out_specs=(vmem, vmem),
        out_shape=(
            jax.ShapeDtypeStruct((LANE_ROWS, PCOLS + 2 * BLK), BF),
            jax.ShapeDtypeStruct((LANE_ROWS, PCOLS), BF),
        ),
        scratch_shapes=[
            pltpu.VMEM((PAD + LANE_ROWS + PAD, STRIP_BLOCKS * BLK), F32),
            pltpu.VMEM((PAD + LANE_ROWS + PAD, BLK), F32),
        ],
        name="local_part",
    )(lane, factor)


def prune_kernel(keep_ref, order_ref, weight_hbm, *rest):
    pieces = rest[:LANES]
    part_refs = rest[LANES : 2 * LANES]
    kept_ref, factor_ref, errors_ref, weight_ref, sems = rest[2 * LANES :]
    copies = [pltpu.make_async_copy(weight_hbm, weight_ref, sems.at[LANES])]
    for place in range(LANES):
        start = pl.multiple_of(order_ref[place] * LANE_ROWS, 16)
        copies.append(
            pltpu.make_async_copy(pieces[place], factor_ref.at[pl.ds(start, LANE_ROWS), :], sems.at[place])
        )
    for copy in copies:
        copy.start()
    for copy in copies:
        copy.wait()
    row = lax.broadcasted_iota(jnp.int32, (BLK, BLK), 0)
    column = lax.broadcasted_iota(jnp.int32, (BLK, BLK), 1)
    eye = (row == column).astype(F32)
    for block in range(NBLK):
        at = block * BLK
        edge = (at // LANE_ROWS + 1) * LANE_ROWS - at
        if edge < BLK:
            stored = factor_ref[at : at + BLK, PCOLS:]
            whole = stored[:, :BLK].astype(F32) + stored[:, BLK:].astype(F32)
            top = jnp.where(row < edge, whole, eye)
            bottom = jnp.where(row < edge, eye, whole)
            factor_ref[at : at + BLK, PCOLS:] = jnp.concatenate(split(mm_split(top, bottom)), axis=1)
    for low in range(0, PCOLS, 2 * BLK):
        width = min(2 * BLK, PCOLS - low)
        current = weight_ref[:, low : low + width].astype(F32)
        if low:
            current = current - jnp.dot(
                errors_ref[:, :low], factor_ref[:low, low : low + width], preferred_element_type=F32
            )
        for half in range(width // BLK):
            at = low + half * BLK
            part = current[:, half * BLK : (half + 1) * BLK]
            if half:
                part = part - jnp.dot(
                    errors_ref[:, low : low + BLK],
                    factor_ref[low : low + BLK, at : at + BLK],
                    preferred_element_type=F32,
                )
            high, lowpart = split(part)
            right = factor_ref[at : at + BLK, PCOLS:]
            both = jnp.dot(
                jnp.concatenate([high, lowpart], axis=1),
                jnp.concatenate([right, right], axis=0),
                preferred_element_type=F32,
            )
            solved = (both[:, :BLK] + both[:, BLK:]).astype(BF)
            for group in range(ROWS_DEV // BLK):
                top = group * BLK
                keep = keep_ref[group, at // BLK] > 0
                error = jnp.where(keep, jnp.zeros((BLK, BLK), BF), solved[top : top + BLK])
                errors_ref[top : top + BLK, at : at + BLK] = error
                part_refs[group][:, at : at + BLK] = error
                kept_ref[top : top + BLK, at : at + BLK] = jnp.where(
                    keep, high[top : top + BLK], jnp.zeros((BLK, BLK), BF)
                )


def prune(keep_mask, order, weight, pieces):
    vmem = pl.BlockSpec(memory_space=pltpu.VMEM)
    smem = pl.BlockSpec(memory_space=pltpu.SMEM)
    hbm = pl.BlockSpec(memory_space=pl.ANY)
    part = jax.ShapeDtypeStruct((BLK, PCOLS), BF)
    return pl.pallas_call(
        prune_kernel,
        in_specs=[smem, smem, hbm] + [hbm] * LANES,
        out_specs=(vmem,) * (LANES + 1),
        out_shape=(part,) * LANES + (jax.ShapeDtypeStruct((ROWS_DEV, PCOLS), BF),),
        scratch_shapes=[
            pltpu.VMEM((PCOLS, PCOLS + 2 * BLK), BF),
            pltpu.VMEM((ROWS_DEV, PCOLS), BF),
            pltpu.VMEM((ROWS_DEV, PCOLS), BF),
            pltpu.SemaphoreType.DMA((LANES + 1,)),
        ],
        name="prune",
    )(keep_mask, order, weight, *pieces)


def subtract(piece, factor, weight_ref, kept_ref, owner):
    product = jnp.dot(piece, factor, preferred_element_type=F32)
    trailing = (weight_ref[...].astype(F32) - product).astype(BF)
    return jnp.where(owner > 0, kept_ref[...], trailing)


def own_kernel(at_ref, first_ref, second_ref, token_ref, *rest):
    parts = rest[:LANES]
    weight_ref, kept_ref, out_ref, factor_ref = rest[LANES:]
    for place, part in enumerate(parts):
        start = pl.multiple_of(at_ref[2 + place] * LANE_ROWS, 16)
        factor_ref[pl.ds(start, part.shape[0]), :] = part[...]
    piece = jnp.concatenate([first_ref[...], second_ref[...]], axis=0)
    out_ref[...] = subtract(piece, factor_ref[...], weight_ref, kept_ref, at_ref[1])


def slab_copies(factor_hbm, factor_ref, sems):
    return [
        pltpu.make_async_copy(factor_hbm.at[:, low:high], factor_ref.at[:, low:high], sems.at[place])
        for place, (low, high) in enumerate(SLABS)
    ]


def subtract_slabs(copies, piece, factor_ref, weight_ref, kept_ref, out_ref, owner):
    for copy, (low, high) in zip(copies, SLABS):
        copy.wait()
        product = jnp.dot(piece, factor_ref[:, low:high], preferred_element_type=F32)
        trailing = (weight_ref[:, low:high].astype(F32) - product).astype(BF)
        out_ref[:, low:high] = jnp.where(owner > 0, kept_ref[:, low:high], trailing)


def near_kernel(at_ref, *rest):
    pieces = rest[:4]
    factor_hbm, weight_ref, kept_ref, out_ref, factor_ref, sems = rest[4:]

    @pl.when(pl.program_id(0) == 0)
    def _():
        copies = slab_copies(factor_hbm, factor_ref, sems)
        for copy in copies:
            copy.start()
        piece = jnp.concatenate([pieces[0][...], pieces[1][...]], axis=0)
        subtract_slabs(copies, piece, factor_ref, weight_ref, kept_ref, out_ref, at_ref[2])

    @pl.when(pl.program_id(0) == 1)
    def _():
        piece = jnp.concatenate([pieces[2][...], pieces[3][...]], axis=0)
        out_ref[...] = subtract(piece, factor_ref[...], weight_ref, kept_ref, at_ref[2])


def far_kernel(at_ref, *rest):
    pieces = rest[:4]
    factor_hbm, weight_ref, kept_ref, out_ref, factor_ref, sems, piece_ref = rest[4:]
    copies = slab_copies(factor_hbm, factor_ref, sems)
    for copy in copies:
        copy.start()
    for place, part_ref in enumerate(pieces):
        start = pl.multiple_of(at_ref[2 + place] * FORWARD, FORWARD)
        piece_ref[pl.ds(start, FORWARD), :] = part_ref[...]
    subtract_slabs(copies, piece_ref[...], factor_ref, weight_ref, kept_ref, out_ref, at_ref[1])


def finish(kernel, steps, at, inputs, weight, kept, extra=None, scratch=(), slabs=False):
    block = pl.BlockSpec((QUARTER, PCOLS), lambda i, at_ref: (at_ref[i], 0))
    vmem = pl.BlockSpec(memory_space=pltpu.VMEM)
    out_shape = [jax.ShapeDtypeStruct((ROWS_DEV, PCOLS), BF)]
    specs = [vmem] * len(inputs)
    if slabs:
        specs[-1] = pl.BlockSpec(memory_space=pl.ANY)
        scratch = (pltpu.VMEM((PCOLS, PCOLS), BF), pltpu.SemaphoreType.DMA((len(SLABS),)), *scratch)
    if extra is not None:
        out_shape.append(extra)
    return pl.pallas_call(
        kernel,
        grid_spec=pltpu.PrefetchScalarGridSpec(
            num_scalar_prefetch=1,
            grid=(steps,),
            in_specs=specs + [block, block],
            out_specs=[block] + [vmem] * (len(out_shape) - 1),
            scratch_shapes=list(scratch),
        ),
        out_shape=out_shape,
        input_output_aliases={len(inputs) + 2: 0},
    )(at, *inputs, weight, kept)


def col_at(x, zh, core):
    return (x % 4) * 8 + (zh % 4) * 2 + core


def row_at(y, zl):
    return (y % 4) * 2 + zl


def vector(value):
    return jnp.reshape(value, (1,)).astype(jnp.int32)


def per_device(weight, factor, keep_mask):
    section = lax.axis_index("col")
    lane = lax.axis_index("row")
    x_at = section // 8
    zh_at = (section // 2) % 4
    core_at = section % 2
    payload, factor_low = local_part(vector(lane), factor)

    def hop(array, dy, flip):
        pairs = [(row_at(y, zl), row_at(y + dy, zl ^ flip)) for y in range(4) for zl in (0, 1)]
        return lax.ppermute(array, ("col", "row"), pairs)

    y_at, zl_at = lane // 2, lane % 2
    up_same = hop(payload, 1, 0)
    down_other = hop(payload, 3, 1)
    up_other = hop(payload, 1, 1)
    down_same = hop(payload, 3, 0)
    other = hop(payload, 0, 1)
    far_same = hop(up_same, 1, 0)
    far_other = hop(down_other, 3, 0)
    pieces = [payload, up_same, down_other, up_other, down_same, other, far_same, far_other]
    order = [
        lane,
        row_at(y_at + 3, zl_at),
        row_at(y_at + 1, 1 - zl_at),
        row_at(y_at + 3, 1 - zl_at),
        row_at(y_at + 1, zl_at),
        row_at(y_at, 1 - zl_at),
        row_at(y_at + 2, zl_at),
        row_at(y_at + 2, 1 - zl_at),
    ]
    *parts_out, kept = prune(keep_mask, jnp.stack(order).astype(jnp.int32), weight, pieces)

    def along(array, dy, flip=0):
        pairs = [
            (c * LANES + row_at(y, zl), c * LANES + row_at(y + dy, zl ^ flip))
            for c in range(1, 32)
            for y in range(4)
            for zl in (0, 1)
        ]
        return lax.ppermute(array, ("col", "row"), pairs)

    token = lax.ppermute(factor_low[:16, :BLK], "col", [(0, 1)])
    partner = along(factor_low, 0, 1)
    even = jnp.where(zl_at == 0, factor_low, partner)
    odd = jnp.where(zl_at == 0, partner, factor_low)
    even_up = along(even, 1)
    odd_down = along(odd, 3)
    odd_up = along(odd, 1)
    even_down = along(even, 3)
    even_far = along(even_up, 1)
    odd_far = along(odd_down, 3)
    parts = (even, odd, even_up, odd_up, even_down, odd_down, even_far, odd_far)
    part_rows = [row_at(y_at + dy, zl) for dy in (0, 3, 1, 2) for zl in (0, 1)]

    places = [(x, z) for x in range(4) for z in range(4)]
    share = [(col_at(x, z, 0), col_at(x, z, 1)) for x, z in places]
    swap = [(col_at(x, z, c), col_at(x, z, 1 - c)) for x, z in places for c in (0, 1)]
    ring = [(col_at(x, z, 0), col_at(x + 1, z, 0)) for x, z in places]
    ring += [(col_at(x, z, 1), col_at(x - 1, z, 1)) for x, z in places]
    owns, nears, near_others, fars, far_others = [], [], [], [], []
    for chunk in (0, 1):
        got = None
        for k in (2, 1, 3):
            sent = lax.ppermute(parts_out[2 * k + chunk], "col", [(0, col_at(k, 0, 0))])
            got = sent if got is None else got + sent
        own = jnp.where(x_at == 0, parts_out[chunk], got)
        up = lax.ppermute(own, "col", [(col_at(x, 0, 0), col_at(x, 1, 0)) for x in range(4)])
        down = lax.ppermute(own, "col", [(col_at(x, 0, 0), col_at(x, 3, 0)) for x in range(4)])
        side, array = ((1, up), (3, down))[chunk]
        far_z = lax.ppermute(array, "col", [(col_at(x, side, 0), col_at(x, 2, 0)) for x in range(4)])
        own = jnp.where(zh_at == 0, own, up + down + far_z)

        shared = lax.ppermute(own, "col", share)
        own = jnp.where(core_at == 0, own, shared)
        near = lax.ppermute(own, "col", ring)
        onward = lax.dynamic_slice(near, (core_at * FORWARD, 0), (FORWARD, PCOLS))
        far = lax.ppermute(onward, "col", ring)
        owns.append(own)
        nears.append(near)
        fars.append(far)
        near_others.append(lax.ppermute(near, "col", swap))
        far_others.append(lax.ppermute(far, "col", swap))

    def ints(*values):
        return jnp.stack([jnp.asarray(value) for value in values]).astype(jnp.int32)

    owner = section == 0
    factor_shape = jax.ShapeDtypeStruct((PCOLS, PCOLS), BF)
    out, factor_all = finish(
        own_kernel, 1, ints(x_at, owner, *part_rows), (*owns, token, *parts), weight, kept, factor_shape
    )
    ways = ints((x_at + 3 - 2 * core_at) % 4, (x_at + 1 + 2 * core_at) % 4, owner)
    (out,) = finish(near_kernel, 2, ways, (*nears, *near_others, factor_all), weight, out, slabs=True)
    (out,) = finish(
        far_kernel,
        1,
        ints((x_at + 2) % 4, owner, core_at, 2 + core_at, 1 - core_at, 3 - core_at),
        (*fars, *far_others, factor_all),
        weight,
        out,
        scratch=[pltpu.VMEM((QUARTER, PCOLS), BF)],
        slabs=True,
    )
    return out


def solution(mesh):
    in_specs = (P("row", "col"), P("row", "col"), P("row", None))
    out_specs = P("row", "col")
    return jax.shard_map(
        per_device, mesh=mesh, in_specs=in_specs, out_specs=out_specs, check_vma=False
    )
```
